32 devices in a mesh: dp: 8 (over z, y), tensor: 4 (over x, core).
Axes of the slice: x: 2, y: 2, z: 4, core: 2. Of those that a mesh axis runs over, the one named last changes fastest.
Arguments:
- tokens: bfloat16 [16384, 2048], P(('dp', 'tensor')), may hold values from -6 to 6
- cotangent: bfloat16 [16384, 2048], P(('dp', 'tensor')), may hold values from -6 to 6
- lengths: int32 [16, 4], replicated, may hold values from 1 to 896, 1024 in all within a row
- sequence_adapter_index: int32 [16, 4], replicated, may hold values from 0 to 7
- deal: int32 [16], replicated, may hold values from 0 to 15, each once
- input_norm_gain: float32 [2048], replicated, may hold values from 0.5 to 1.5
- inner_projection_weight: bfloat16 [2048, 2, 4096], P(None, None, 'tensor'), may hold values from -0.125 to 0.125
- state_projection_weight: bfloat16 [2048, 256], replicated, may hold values from -0.125 to 0.125
- step_projection_weight: bfloat16 [2048, 64], P(None, 'tensor'), may hold values from -0.125 to 0.125
- inner_conv_taps: float32 [5, 4096], P(None, 'tensor'), may hold values from -3 to 3
- state_conv_taps: float32 [5, 256], replicated, may hold values from -3 to 3
- head_parameters: float32 [3, 64], P(None, 'tensor'), may hold values from -14 to 3, as said below
- gated_norm_gain: float32 [4096], P('tensor'), may hold values from 0.5 to 1.5
- output_projection_weight: bfloat16 [4096, 2048], P('tensor'), may hold values from -0.09375 to 0.09375
- adapter_input_down: bfloat16 [2048, 8, 16], replicated, may hold values from -0.125 to 0.125
- adapter_input_up: bfloat16 [8, 16, 2, 4096], P(None, None, None, 'tensor'), may hold values from -1 to 1
- adapter_output_down: bfloat16 [4096, 8, 16], P('tensor'), may hold values from -0.09375 to 0.09375
- adapter_output_up: bfloat16 [8, 16, 2048], replicated, may hold values from -1 to 1
Outputs:
- output: bfloat16 [16384, 2048], P(('dp', 'tensor'))
- grad_in: float32 [16384, 2048], P(('dp', 'tensor'))
- grad_in_down: float32 [2048, 8, 16], replicated
- input_up_gradient: float32 [8, 16, 2, 4096], P(None, None, None, 'tensor')
- grad_out_down: float32 [4096, 8, 16], P('tensor')
- output_up_gradient: float32 [8, 16, 2048], replicated
The draws below stay inside these ranges and needn't reach their ends.
Inputs may be any that keep to these rules, and one draw needn't show every extreme that they name: `lengths`: each row sums to 1024, and each row has one sequence of exactly 896. `deal`: a permutation of the packed rows. `head_parameters`: row 0 is the step bias, row 1 the logarithm of the decay rate (0 to log 16), row 2 the skip gain (0.5 to 1.5).
All inputs are finite; a program needn't handle non-finite values.
Results may differ from the reference program's by a relative error of at most 0.012.
Values may be sent and summed in bfloat16 or wider, within the bound.
A program may use at most 256 MiB of HBM per device.

```python
import math
import jax
import jax.numpy as jnp
import numpy as np
from jax import lax

MODEL_WIDTH = 2048
H = 64
P_SIZE = 64
N = 128
KW = 4
BLOCK = 256
ADAPTER_TOTAL = 8
ADAPTER_RANK = 16
ROW_LEN = 1024
SEGS = 4
MOSTLEN = 896
RPD = 2
INNER_CHANNELS = 4096
NROWS = 16
NTOK = 16384


def draw_head_parameters(key, part):
    key_rate, key_scale, key_skip = jax.random.split(jax.random.fold_in(key, 11), 3)
    low_end = math.log(1.0 / (4.0 * MOSTLEN))
    high_end = math.log(1.0 / 30.0)
    log_rate = jax.random.uniform(key_rate, (H,), jnp.float32, low_end, high_end)
    log_scale = jax.random.uniform(key_scale, (H,), jnp.float32, 0.0, math.log(16.0))
    skip_gain = jax.random.uniform(key_skip, (H,), jnp.float32, 0.5, 1.5)
    step_bias = log_rate - 0.5 - log_scale
    return jnp.stack([step_bias, log_scale, skip_gain], axis=0)


def set_ends(entries, stream_key, low, high):
    longest = entries.shape.index(max(entries.shape))
    spots = []
    for shift in (0, 1):
        where = [jax.random.randint(jax.random.fold_in(stream_key, axis), (), 0, length) for axis, length in enumerate(entries.shape)]
        where[longest] = (where[longest] + shift) % entries.shape[longest]
        spots.append(tuple(where))
    return entries.at[spots[0]].set(low).at[spots[1]].set(high)


def shard_levels(key, extent, cuts, low, high):
    def one(dim, blocks):
        heights = jax.random.uniform(jax.random.fold_in(jax.random.fold_in(key, 6), dim), (blocks,), jnp.float32, low / len(cuts), high / len(cuts))
        return jnp.repeat(jnp.exp(heights), extent[dim] // blocks).reshape((-1,) + (1,) * (len(extent) - dim - 1))

    factor_of = one(*cuts[0])
    for cut in cuts[1:]:
        factor_of = factor_of * one(*cut)
    return factor_of


def split_up(amount, total, bound, lean):
    loads = [(1 << 20) // math.isqrt(standing ** lean) + 1 for standing in range(2, amount + 1)]
    rest, given = total - bound - (amount - 1), [1] * (amount - 1)
    while rest > 0:
        candidates = [i for i in range(amount - 1) if given[i] < bound]
        mass, budget = sum([loads[i] for i in candidates]), rest
        for i in candidates:
            more = min(bound - given[i], max(1, budget * loads[i] // mass), rest)
            given[i] = given[i] + more
            rest = rest - more
    return np.array([bound] + given)


def ragged_sizes(key, count, total, reach, lean):
    if count == 2:
        one = jax.random.randint(key, (), max(1, total - reach), min(reach, total - 1) + 1)
        return jnp.stack([one, total - one])
    sizes = jnp.asarray(split_up(count, total, reach, lean), jnp.int32)
    pairs = (count - 1) // 2
    donor, receiver = sizes[1:1 + 2 * pairs:2], sizes[2:2 + 2 * pairs:2]
    slack = jnp.minimum(donor - 1, reach - receiver)
    moved = jax.random.randint(jax.random.fold_in(key, 1), (pairs,), 0, 1 << 20) % (slack + 1)
    sizes = sizes.at[1:1 + 2 * pairs:2].set(donor - moved).at[2:2 + 2 * pairs:2].set(receiver + moved)
    return sizes[jax.random.permutation(jax.random.fold_in(key, 2), count)]


def normal_values(rng, shape, deviation, bound, cuts=(), kind=jnp.bfloat16):
    drawn = deviation * jax.random.normal(rng, shape, jnp.float32)
    if cuts:
        drawn = drawn * shard_levels(rng, shape, cuts, -0.22, 0.18)
    return jnp.clip(drawn, -bound, bound).astype(kind)


def setup_inputs(seed: int = 0) -> dict:
    seeds = jax.random.split(jax.random.key(seed), 19)
    return {
        "tokens": normal_values(seeds[0], (NTOK, MODEL_WIDTH), 1.0, 6.0, ((0, 32),)),
        "cotangent": normal_values(seeds[1], (NTOK, MODEL_WIDTH), 1.0, 6.0, ((0, 32),)),
        "lengths": jax.vmap(lambda own: ragged_sizes(own, SEGS, ROW_LEN, MOSTLEN, 0))(jax.random.split(seeds[2], NROWS)).reshape((NROWS, SEGS)).astype(jnp.int32),
        "sequence_adapter_index": set_ends(jax.random.randint(seeds[3], (NROWS, SEGS), 0, ADAPTER_TOTAL), jax.random.fold_in(seeds[3], 1), 0, ADAPTER_TOTAL - 1).astype(jnp.int32),
        "deal": jax.random.permutation(seeds[4], NROWS).astype(jnp.int32),
        "input_norm_gain": jnp.clip(1.0 + 0.1 * jax.random.normal(seeds[5], (MODEL_WIDTH,), jnp.float32), 0.5, 1.5),
        "inner_projection_weight": normal_values(seeds[6], (MODEL_WIDTH, 2, INNER_CHANNELS), MODEL_WIDTH ** -0.5, 0.125, ((2, 4),)),
        "state_projection_weight": normal_values(seeds[7], (MODEL_WIDTH, 2 * N), MODEL_WIDTH ** -0.5, 0.125),
        "step_projection_weight": normal_values(seeds[8], (MODEL_WIDTH, H), MODEL_WIDTH ** -0.5, 0.125, ((1, 4),)),
        "inner_conv_taps": normal_values(seeds[9], (KW + 1, INNER_CHANNELS), 0.5, 3.0, ((1, 4),), jnp.float32),
        "state_conv_taps": normal_values(seeds[10], (KW + 1, 2 * N), 0.5, 3.0, (), jnp.float32),
        "head_parameters": draw_head_parameters(jax.random.fold_in(seeds[18], 71), 0),
        "gated_norm_gain": jnp.clip(1.0 + 0.1 * jax.random.normal(seeds[12], (INNER_CHANNELS,), jnp.float32), 0.5, 1.5),
        "output_projection_weight": normal_values(seeds[13], (INNER_CHANNELS, MODEL_WIDTH), INNER_CHANNELS ** -0.5, 0.09375, ((0, 4),)),
        "adapter_input_down": normal_values(seeds[14], (MODEL_WIDTH, ADAPTER_TOTAL, ADAPTER_RANK), MODEL_WIDTH ** -0.5, 0.125),
        "adapter_input_up": normal_values(seeds[15], (ADAPTER_TOTAL, ADAPTER_RANK, 2, INNER_CHANNELS), (0.25 * ADAPTER_RANK ** -0.5), 1.0, ((3, 4),)),
        "adapter_output_down": normal_values(seeds[16], (INNER_CHANNELS, ADAPTER_TOTAL, ADAPTER_RANK), INNER_CHANNELS ** -0.5, 0.09375, ((0, 4),)),
        "adapter_output_up": normal_values(seeds[17], (ADAPTER_TOTAL, ADAPTER_RANK, MODEL_WIDTH), (0.25 * ADAPTER_RANK ** -0.5), 1.0),
    }


epsilon = 1e-05
top_precision = lax.Precision.HIGHEST

@jax.custom_vjp
def reduced_rank(v):
    return lax.optimization_barrier(v.astype(jnp.bfloat16)).astype(jnp.float32)

@jax.custom_vjp
def reduced_backward(v):
    return v

def low_keep(v):
    return (reduced_rank(v), None)

def low_pass(kept, grad):
    return (grad,)

def back_keep(v):
    return (v, None)

def back_low(kept, grad):
    return (reduced_rank(grad),)
reduced_rank.defvjp(low_keep, low_pass)
reduced_backward.defvjp(back_keep, back_low)

def segment_info(lengths_rows, ids_rows, row_length):
    ends = jnp.cumsum(lengths_rows, axis=1).astype(jnp.int32)
    starts = (ends - lengths_rows).astype(jnp.int32)
    position = jnp.arange(row_length, dtype=jnp.int32)
    segment = lax.optimization_barrier(jnp.sum((position[None, :, None] >= ends[:, None, :]).astype(jnp.int32), axis=2)).astype(jnp.int32)
    member = segment[:, :, None] == jnp.arange(lengths_rows.shape[1], dtype=jnp.int32)[None, None, :]
    begins = lax.optimization_barrier(jnp.sum(jnp.where(member, starts[:, None, :], 0), axis=2)).astype(jnp.int32)
    within = (position[None, :] - begins).astype(jnp.int32)
    adapter = lax.optimization_barrier(jnp.sum(jnp.where(member, ids_rows[:, None, :], 0), axis=2)).astype(jnp.int32)
    return (segment, within, adapter)

def selection(adapter, number_of_adapters, adapter_rank_width):
    column = (jnp.arange(number_of_adapters * adapter_rank_width, dtype=jnp.int32) // adapter_rank_width).astype(jnp.int32)
    return (adapter.reshape(-1, 1) == column[None, :]).astype(jnp.float32)

def causal_conv(values, taps, within):
    seq_len = values.shape[1]
    tap_count = taps.shape[0] - 1
    summed = taps[tap_count] + jnp.zeros_like(values)
    for lag_steps in range(tap_count):
        shifted = jnp.pad(values, ((0, 0), (lag_steps, 0), (0, 0)))[:, :seq_len]
        usable = (within >= lag_steps)[:, :, None]
        summed = summed + jnp.where(usable, shifted, 0.0) * taps[tap_count - 1 - lag_steps]
    return jax.nn.silu(summed)

def state_scan(weighted, log_decay, input_mat, output_mat, segment, block_len):
    seq_rows, seq_len, head_count, head_size = weighted.shape
    block_count = seq_len // block_len

    def split_blocks(array_in):
        return jnp.moveaxis(array_in.reshape((seq_rows, block_count, block_len) + array_in.shape[2:]), 1, 0)
    inputs = tuple((split_blocks(member_array) for member_array in (weighted, log_decay, input_mat, output_mat, segment)))
    start_state = jnp.zeros((seq_rows, head_count, head_size, input_mat.shape[2]), jnp.float32)
    start_prev = jnp.full((seq_rows,), -1, jnp.int32)
    lower_tri = jnp.tril(jnp.ones((block_len, block_len), jnp.bool_))

    def advance(carried_in, block_data):
        state, previous = carried_in
        xdt, decay_blk, in_blk, out_blk, seg_blk = block_data
        cumul = jnp.cumsum(decay_blk, axis=1)
        allowed = (seg_blk[:, :, None] == seg_blk[:, None, :]) & lower_tri[None]
        allowed = allowed[..., None]
        spread = cumul[:, :, None, :] - cumul[:, None, :, :]
        weights = jnp.where(allowed, jnp.exp(jnp.where(allowed, spread, 0.0)), 0.0)
        scores = jnp.einsum('rin,rjn->rij', out_blk, in_blk, precision=top_precision)
        inside = jnp.einsum('rijh,rjhp->rihp', weights * scores[..., None], xdt, precision=top_precision)
        carried = jnp.where((seg_blk == previous[:, None])[..., None], jnp.exp(cumul), 0.0)
        inside = inside + jnp.einsum('rin,rhpn->rihp', out_blk, state, precision=top_precision) * carried[..., None]
        last_seg = seg_blk[:, -1]
        tail_w = jnp.where((seg_blk == last_seg[:, None])[..., None], jnp.exp(cumul[:, -1:, :] - cumul), 0.0)
        keep_w = jnp.where((last_seg == previous)[:, None], jnp.exp(cumul[:, -1, :]), 0.0)
        state = keep_w[:, :, None, None] * state + jnp.einsum('rjh,rjn,rjhp->rhpn', tail_w, in_blk, xdt, precision=top_precision)
        return ((state, last_seg), inside)
    final_carry, outputs = lax.scan(jax.checkpoint(advance), (start_state, start_prev), inputs)
    return jnp.moveaxis(outputs, 0, 1).reshape(seq_rows, seq_len, head_count, head_size)

def mixer(gate_inner_projection, proj_bc, proj_dt, inner_conv_taps, state_conv_taps, head_parameters, segment, within, head_size, block_len):
    gate_in = gate_inner_projection[:, :, 0, :]
    inner_in = gate_inner_projection[:, :, 1, :]
    conv_out = causal_conv(inner_in, inner_conv_taps, within)
    state_io = causal_conv(proj_bc, state_conv_taps, within)
    state_dim = proj_bc.shape[2] // 2
    input_mat = state_io[:, :, :state_dim]
    output_mat = state_io[:, :, state_dim:]
    step_size = jax.nn.softplus(proj_dt + head_parameters[0])
    log_decay = -jnp.exp(head_parameters[1]) * step_size
    seq_rows, seq_len, channel_width = conv_out.shape
    head_count = channel_width // head_size
    values = conv_out.reshape(seq_rows, seq_len, head_count, head_size)
    result = state_scan(values * step_size[..., None], log_decay, input_mat, output_mat, segment, block_len)
    result = result + head_parameters[2][:, None] * values
    return result.reshape(seq_rows, seq_len, channel_width) * jax.nn.silu(gate_in)

def layer(tokens_in, adapter_tables, frozen, segment, within, adapter_selector):
    first_inner_factor, second_inner_factor, first_outer_factor, second_outer_factor = adapter_tables
    input_norm_gain, inner_projection_weight, state_projection_weight, step_projection_weight, inner_conv_taps, state_conv_taps, head_parameters, gated_norm_gain, output_projection_weight = frozen
    seq_rows, seq_len, model_width = tokens_in.shape
    flat_tokens = tokens_in.reshape(seq_rows * seq_len, model_width)
    normalized_input = flat_tokens * lax.rsqrt(lax.optimization_barrier(jnp.mean(flat_tokens * flat_tokens, axis=1, keepdims=True)) + epsilon) * input_norm_gain
    normalized_input = reduced_rank(normalized_input)
    reduced_count = first_inner_factor.shape[1] * first_inner_factor.shape[2]
    adapter_middle = reduced_rank(reduced_backward(jnp.dot(normalized_input, first_inner_factor.reshape(model_width, reduced_count), precision=top_precision) * adapter_selector))
    gate_inner_projection = jnp.dot(normalized_input, inner_projection_weight.reshape(model_width, -1), precision=top_precision) + jnp.dot(adapter_middle, second_inner_factor.reshape(reduced_count, -1), precision=top_precision)
    gate_inner_projection = reduced_backward(gate_inner_projection)
    proj_bc = reduced_backward(jnp.dot(normalized_input, state_projection_weight, precision=top_precision))
    proj_dt = reduced_backward(jnp.dot(normalized_input, step_projection_weight, precision=top_precision))
    channel_width = inner_projection_weight.shape[2]
    gated = mixer(gate_inner_projection.reshape(seq_rows, seq_len, 2, channel_width), proj_bc.reshape(seq_rows, seq_len, -1), proj_dt.reshape(seq_rows, seq_len, -1), inner_conv_taps, state_conv_taps, head_parameters, segment, within, P_SIZE, BLOCK).reshape(seq_rows * seq_len, channel_width)
    factor = lax.rsqrt(lax.optimization_barrier(jnp.mean(gated * gated, axis=1, keepdims=True)) + epsilon)
    mixer_input = reduced_rank(gated * factor * gated_norm_gain)
    adapter_backward = reduced_rank(reduced_backward(jnp.dot(mixer_input, first_outer_factor.reshape(channel_width, reduced_count), precision=top_precision) * adapter_selector))
    adapter_update = jnp.dot(mixer_input, output_projection_weight, precision=top_precision) + jnp.dot(adapter_backward, second_outer_factor.reshape(reduced_count, model_width), precision=top_precision)
    return (flat_tokens + adapter_update).reshape(seq_rows, seq_len, model_width)

def reference(tokens, cotangent, lengths, sequence_adapter_index, deal, input_norm_gain, inner_projection_weight, state_projection_weight, step_projection_weight, inner_conv_taps, state_conv_taps, head_parameters, gated_norm_gain, output_projection_weight, adapter_input_down, adapter_input_up, adapter_output_down, adapter_output_up):
    group_count = NROWS // RPD
    frozen = (input_norm_gain, inner_projection_weight.astype(jnp.float32), state_projection_weight.astype(jnp.float32), step_projection_weight.astype(jnp.float32), inner_conv_taps, state_conv_taps, head_parameters, gated_norm_gain, output_projection_weight.astype(jnp.float32))
    adapter_tables = (adapter_input_down.astype(jnp.float32), adapter_input_up.astype(jnp.float32), adapter_output_down.astype(jnp.float32), adapter_output_up.astype(jnp.float32))
    tok_groups = tokens.reshape(group_count, RPD, ROW_LEN, MODEL_WIDTH)
    cot_groups = cotangent.reshape(group_count, RPD, ROW_LEN, MODEL_WIDTH)
    dealt_len = jnp.take(lengths, deal, axis=0).reshape(group_count, RPD, SEGS)
    dealt_ids = jnp.take(sequence_adapter_index, deal, axis=0).reshape(group_count, RPD, SEGS)
    zero_grads = tuple((jnp.zeros_like(array_in) for array_in in adapter_tables))

    def per_group(sums, group_data):
        tok_group, cot_group, len_group, id_group = group_data
        segment, within, adapter = segment_info(len_group, id_group, ROW_LEN)
        adapter_selector = selection(adapter, ADAPTER_TOTAL, ADAPTER_RANK)

        def forward(tokens_f, adapter_f):
            return layer(tokens_f, adapter_f, frozen, segment, within, adapter_selector)
        result, pullback = jax.vjp(forward, tok_group.astype(jnp.float32), adapter_tables)
        grad_tokens, grad_adapters = pullback(cot_group.astype(jnp.float32))
        sums = tuple((old_sum + new_term for old_sum, new_term in zip(sums, grad_adapters)))
        return (sums, (result.astype(jnp.bfloat16), grad_tokens))
    sums, (outputs, grads) = lax.scan(per_group, zero_grads, (tok_groups, cot_groups, dealt_len, dealt_ids))
    return (outputs.reshape(NTOK, MODEL_WIDTH), grads.reshape(NTOK, MODEL_WIDTH), sums[0], sums[1], sums[2], sums[3])
```

```python
import functools

import jax
import jax.numpy as jnp
from jax import lax
from jax.experimental import pallas as pl
from jax.experimental.pallas import tpu as pltpu
from jax.sharding import PartitionSpec as P

F32, BF16 = jnp.float32, jnp.bfloat16
L = 128
HEAD = 64
HALO = 8
NN = (((1,), (0,)), ((), ()))
NT = (((1,), (1,)), ((), ()))
TN = (((0,), (0,)), ((), ()))


def mm(a, b, dims=NN):
    return lax.dot_general(a, b, dims, preferred_element_type=F32)


def split2(v):
    hi = v.astype(BF16)
    return hi, (v - hi.astype(F32)).astype(BF16)


def split3(v):
    hi = v.astype(BF16)
    rest = v - hi.astype(F32)
    mid = rest.astype(BF16)
    return hi, mid, (rest - mid.astype(F32)).astype(BF16)


def sigmoid(v):
    return 0.5 * jnp.tanh(0.5 * v) + 0.5


def starts_of(pos, ends, count):
    start = jnp.zeros_like(pos)
    for k in range(count - 1):
        start = jnp.where(pos >= ends[k], jnp.maximum(start, ends[k]), start)
    return start


def scalar_start(pos, ends, count):
    start = jnp.int32(0)
    for k in range(count - 1):
        start = jnp.where(pos >= ends[k], jnp.maximum(start, ends[k]), start)
    return start


def chunk_geometry(t0, ends, count):
    rows = t0 + lax.broadcasted_iota(jnp.int32, (L, L), 0)
    cols = t0 + lax.broadcasted_iota(jnp.int32, (L, L), 1)
    row_start = starts_of(rows, ends, count)
    col_start = starts_of(cols, ends, count)
    last_start = scalar_start(t0 + (L - 1), ends, count)
    return rows, cols, row_start, col_start, last_start


def conv_tile(ext, taps, within):
    total = ext[HALO:] * taps[3:4] + taps[4:5]
    for lag in range(1, 4):
        moved = pltpu.roll(ext, lag, 0)[HALO:]
        total = total + jnp.where(within >= lag, moved, 0.0) * taps[3 - lag : 4 - lag]
    return total


def conv_back(ext, taps, ok):
    size = ext.shape[0]
    total = ext[:L] * taps[3:4]
    for lag in range(1, 4):
        moved = pltpu.roll(ext, size - lag, 0)[:L]
        total = total + jnp.where(ok[lag - 1], moved, 0.0) * taps[3 - lag : 4 - lag]
    return total


def step_terms(dt_raw, bias, rate, low_mask):
    raw = dt_raw + bias
    dt = jnp.maximum(raw, 0.0) + jnp.log1p(jnp.exp(-jnp.abs(raw)))
    decay = dt * rate
    cum = sum(mm(low_mask, part) for part in split3(decay))
    return raw, dt, cum


def lane_pair(low, value, h):
    first = jnp.broadcast_to(value[:, h : h + 1], (L, 128))
    second = jnp.broadcast_to(value[:, h + 1 : h + 2], (L, 128))
    return first, second, jnp.where(low, first, second)


def forward_kernel(
    count, ends, z_ref, x_ref, bc_ref, dt_ref, taps_ref, bct_ref, head_ref, chan_ref,
    y_ref, g_ref, sum_ref, st_ref, state, xprev, bcprev,
):
    c = pl.program_id(0)
    pairs = x_ref.shape[1] // 128

    @pl.when(c == 0)
    def _():
        state[...] = jnp.zeros_like(state)
        xprev[...] = jnp.zeros_like(xprev)
        bcprev[...] = jnp.zeros_like(bcprev)

    t0 = c * L
    rows, cols, row_start, col_start, last_start = chunk_geometry(t0, ends, count)
    within = rows - row_start
    mask = (row_start == col_start) & (cols <= rows)
    low_mask = jnp.where(mask, 1.0, 0.0).astype(BF16)
    contin = row_start < t0
    tail = row_start == last_start
    keep = jnp.where(last_start < t0, 1.0, 0.0).astype(F32)
    low = lax.broadcasted_iota(jnp.int32, (L, 128), 1) < HEAD

    bc_halves = []
    for half in range(2):
        cut = slice(half * 128, half * 128 + 128)
        ext = jnp.concatenate([bcprev[:, cut], bc_ref[:, cut]], axis=0)
        pre = conv_tile(ext, bct_ref[:, cut], within)
        bc_halves.append((pre * sigmoid(pre)))
    b_mat, c_mat = bc_halves
    b_low, c_low = b_mat.astype(BF16), c_mat.astype(BF16)
    b_turn = b_mat.T.astype(BF16)
    scores = jnp.where(mask, mm(c_low, b_low, NT), 0.0)

    _, dt, cum = step_terms(dt_ref[...], head_ref[0:1], head_ref[1:2], low_mask)
    cum_turn = cum.T

    squares = jnp.zeros((L, 128), F32)
    for p in range(pairs):
        cut = slice(p * 128, p * 128 + 128)
        ext = jnp.concatenate([xprev[:, cut], x_ref[:, cut]], axis=0)
        pre = conv_tile(ext, taps_ref[:, cut], within)
        xc = pre * sigmoid(pre)
        c0, c1, c_both = lane_pair(low, cum, 2 * p)
        _, _, dt_both = lane_pair(low, dt, 2 * p)
        xt = xc * dt_both
        xb = xt.astype(BF16)
        zero = jnp.zeros_like(xb)
        x2 = jnp.concatenate([jnp.where(low, xb, zero), jnp.where(low, zero, xb)], axis=0)
        g0 = (scores * jnp.exp(jnp.minimum(c0 - cum_turn[2 * p : 2 * p + 1], 0.0))).astype(BF16)
        g1 = (scores * jnp.exp(jnp.minimum(c1 - cum_turn[2 * p + 1 : 2 * p + 2], 0.0))).astype(BF16)
        inside = mm(jnp.concatenate([g0, g1], axis=1), x2)
        old = state[:, cut]
        old_low = old.astype(BF16)
        st_ref[0, :, cut] = old_low
        carried = jnp.where(contin, jnp.exp(c_both), 0.0)
        y = inside + mm(c_low, old_low) * carried
        y_ref[:, cut] = y
        c_last = c_both[L - 1 :, :]
        tail_w = jnp.where(tail, jnp.exp(c_last - c_both), 0.0)
        state[:, cut] = (keep * jnp.exp(c_last)) * old + mm(b_turn, (xt * tail_w).astype(BF16))
        z = z_ref[:, cut]
        gated = (y + chan_ref[0:1, cut] * xc) * (z * sigmoid(z))
        gained = gated * chan_ref[1:2, cut]
        g_ref[:, cut] = gained.astype(BF16)
        squares = squares + gated * gated
    ones = jnp.ones((8, 128), BF16)
    sq_row = sum(mm(ones, part, NT) for part in split3(squares))
    sum_ref[...] = sq_row
    xprev[...] = x_ref[L - HALO :, :]
    bcprev[...] = bc_ref[L - HALO :, :]


def backward_kernel(
    count, seq, ends, z_ref, x_ref, xh_ref, bc_ref, bch_ref, dt_ref, gm_ref, y_ref, st_ref, rk_ref,
    taps_ref, bct_ref, head_ref, chan_ref,
    dzx_ref, dbc_ref, ddt_ref, dstate, dnext, dbnext, ends_row,
):
    g = pl.program_id(0)
    c = pl.num_programs(0) - 1 - g
    width = x_ref.shape[1]
    pairs = width // 128

    @pl.when(g == 0)
    def _():
        dstate[...] = jnp.zeros_like(dstate)
        dnext[...] = jnp.zeros_like(dnext)
        dbnext[...] = jnp.zeros_like(dbnext)
        ends_row[...] = jnp.zeros_like(ends_row)

    t0 = c * L
    rows, cols, row_start, col_start, last_start = chunk_geometry(t0, ends, count)
    within = rows - row_start
    same = row_start == col_start
    low_mask = jnp.where(same & (cols <= rows), 1.0, 0.0).astype(BF16)
    up = same & (rows <= cols)
    up_mask = jnp.where(up, 1.0, 0.0).astype(BF16)
    contin = row_start < t0
    tail = row_start == last_start
    keep = jnp.where(last_start < t0, 1.0, 0.0).astype(F32)
    lane = lax.broadcasted_iota(jnp.int32, (L, 128), 1)
    sub = lax.broadcasted_iota(jnp.int32, (L, 128), 0)
    low = lane < HEAD
    ok = [
        (rows + lag < seq) & (starts_of(rows + lag, ends, count) <= rows) for lag in range(1, 4)
    ]

    parts = []
    for half in range(2):
        cut = slice(half * 128, half * 128 + 128)
        ext = jnp.concatenate([bch_ref[:, cut], bc_ref[:, cut]], axis=0)
        pre = conv_tile(ext, bct_ref[:, cut], within)
        sg = sigmoid(pre)
        act = pre * sg
        parts.append((act, sg + act * (1.0 - sg)))
    (b_mat, b_slope), (c_mat, c_slope) = parts
    b_low, c_low = b_mat.astype(BF16), c_mat.astype(BF16)
    c_turn = c_mat.T.astype(BF16)
    scores = jnp.where(up, mm(b_low, c_low, NT), 0.0)

    raw, dt, cum = step_terms(dt_ref[...], head_ref[0:1], head_ref[1:2], low_mask)
    cum_turn = cum.T
    inv, kappa = rk_ref[:, :128], rk_ref[:, 128:]

    d_scores = jnp.zeros((L, L), F32)
    d_b = jnp.zeros((L, 128), F32)
    d_c = jnp.zeros((L, 128), F32)
    d_cum = jnp.zeros((L, 128), F32)
    d_dt = jnp.zeros((L, 128), F32)
    d_end = jnp.zeros((8, 128), F32)
    for p in range(pairs):
        cut = slice(p * 128, p * 128 + 128)
        pick = jnp.where(lane == 2 * p + jnp.where(sub >= HEAD, 1, 0), 1.0, 0.0).astype(BF16)
        ext = jnp.concatenate([xh_ref[:, cut], x_ref[:, cut]], axis=0)
        taps = taps_ref[:, cut]
        pre = conv_tile(ext, taps, within)
        sg = sigmoid(pre)
        xc = pre * sg
        skip = chan_ref[0:1, cut]
        z = z_ref[:, cut]
        sz = sigmoid(z)
        sil = z * sz
        y = y_ref[:, cut]
        yt = y + skip * xc
        gg = inv * (gm_ref[:, cut] * chan_ref[1:2, cut] - kappa * (yt * sil))
        dzx_ref[:, cut] = (gg * yt * (sz + sil * (1.0 - sz))).astype(BF16)
        dyt = gg * sil
        dyb = dyt.astype(BF16)
        zero = jnp.zeros_like(dyb)
        dy2 = jnp.concatenate([jnp.where(low, dyb, zero), jnp.where(low, zero, dyb)], axis=0)
        c0, c1, c_both = lane_pair(low, cum, 2 * p)
        _, _, dt_both = lane_pair(low, dt, 2 * p)
        xt = xc * dt_both
        xb = xt.astype(BF16)
        dg = mm(xb, dy2, NT)
        w0 = jnp.exp(jnp.minimum(cum_turn[2 * p : 2 * p + 1] - c0, 0.0))
        w1 = jnp.exp(jnp.minimum(cum_turn[2 * p + 1 : 2 * p + 2] - c1, 0.0))
        d_scores = d_scores + dg[:, :L] * w0 + dg[:, L:] * w1
        gt = jnp.concatenate([(scores * w0).astype(BF16), (scores * w1).astype(BF16)], axis=1)
        carried = jnp.where(contin, jnp.exp(c_both), 0.0)
        c_last = c_both[L - 1 :, :]
        tail_w = jnp.where(tail, jnp.exp(c_last - c_both), 0.0)
        ds = dstate[:, cut]
        ds_low = ds.astype(BF16)
        dxt = mm(gt, dy2) + mm(b_low, ds_low) * tail_w
        dyc = (dyt * carried).astype(BF16)
        st = st_ref[0, :, cut]
        d_c = d_c + mm(dyc, st, NT)
        d_b = d_b + mm((xt * tail_w).astype(BF16), ds_low, NT)
        ds_new = (keep * jnp.exp(c_last)) * ds + mm(c_turn, dyc)
        dstate[:, cut] = ds_new
        both = jnp.sum(ds_new * st.astype(F32), axis=0, keepdims=True)
        both = jnp.broadcast_to(both, (8, 128))
        d_end = d_end + sum(mm(part, pick) for part in split2(both))
        v = dyb.astype(F32) * y - xb.astype(F32) * dxt
        d_cum = d_cum + sum(mm(part, pick) for part in split2(v))
        d_dt = d_dt + sum(mm(part, pick) for part in split2(dxt * xc))
        dpre = (skip * dyt + dt_both * dxt) * (sg + xc * (1.0 - sg))
        ext = jnp.concatenate([dpre, dnext[:, cut]], axis=0)
        dzx_ref[:, slice(width + p * 128, width + p * 128 + 128)] = conv_back(ext, taps, ok).astype(BF16)
        dnext[:, cut] = dpre[:HALO]

    d_scores = jnp.where(up, d_scores, 0.0)
    d_b = d_b + mm(d_scores.astype(BF16), c_low)
    d_c = d_c + mm(d_scores.T.astype(BF16), b_low)
    for half, (grad, slope) in enumerate(((d_b, b_slope), (d_c, c_slope))):
        cut = slice(half * 128, half * 128 + 128)
        dpre = grad * slope
        ext = jnp.concatenate([dpre, dbnext[:, cut]], axis=0)
        dbc_ref[:, cut] = conv_back(ext, bct_ref[:, cut], ok).astype(BF16)
        dbnext[:, cut] = dpre[:HALO]
    d_cum = d_cum + jnp.where(sub == L - 1, ends_row[0:1, :], 0.0)
    ends_row[...] = d_end
    d_decay = sum(mm(up_mask, part) for part in split3(d_cum))
    ddt_ref[...] = ((d_dt + head_ref[1:2] * d_decay) * sigmoid(raw)).astype(BF16)


def mixer_forward(ends, zx, small, taps, bctaps, heads, chans):
    seq, width = zx.shape[0], zx.shape[1] // 2
    count = ends.shape[0] - 1
    chunks = seq // L
    place = lambda c, e: lax.rem(c + e[count] * (chunks // 2), chunks)
    fixed = lambda shape: pl.BlockSpec(shape, lambda c, e: (0,) * len(shape))
    blk = lambda w, j=0: pl.BlockSpec((L, w), lambda c, e: (place(c, e), j))
    return pl.pallas_call(
        functools.partial(forward_kernel, count),
        grid_spec=pltpu.PrefetchScalarGridSpec(
            num_scalar_prefetch=1,
            grid=(chunks,),
            in_specs=[
                blk(width, 0), blk(width, 1), blk(256, 0), blk(128, 2),
                fixed((5, width)), fixed((5, 256)), fixed((2, 128)), fixed((2, width)),
            ],
            out_specs=[
                blk(width), blk(width), pl.BlockSpec((8, L), lambda c, e: (0, place(c, e))),
                pl.BlockSpec((1, 128, width), lambda c, e: (c, 0, 0)),
            ],
            scratch_shapes=[
                pltpu.VMEM((128, width), F32), pltpu.VMEM((HALO, width), F32), pltpu.VMEM((HALO, 256), F32),
            ],
        ),
        out_shape=[
            jax.ShapeDtypeStruct((seq, width), F32),
            jax.ShapeDtypeStruct((seq, width), BF16),
            jax.ShapeDtypeStruct((8, seq), F32),
            jax.ShapeDtypeStruct((chunks, 128, width), BF16),
        ],
        compiler_params=pltpu.CompilerParams(dimension_semantics=("arbitrary",)),
        cost_estimate=pl.CostEstimate(
            flops=seq * width * 1200, bytes_accessed=seq * width * 16, transcendentals=seq * width * 6
        ),
        name="mixer_forward",
    )(ends, zx, zx, small, small, taps, bctaps, heads, chans)


def mixer_backward(ends, zx, small, gm, y, states, rk, taps, bctaps, heads, chans):
    seq, width = gm.shape
    count = ends.shape[0] - 1
    chunks = seq // L
    last = chunks - 1
    step = L // HALO
    place = lambda c, e: lax.rem(c + e[count] * (chunks // 2), chunks)
    fixed = lambda shape: pl.BlockSpec(shape, lambda g, e: (0,) * len(shape))
    blk = lambda w, j=0: pl.BlockSpec((L, w), lambda g, e: (place(last - g, e), j))
    halo = lambda w, j=0: pl.BlockSpec(
        (HALO, w), lambda g, e: (place(jnp.maximum(last - g - 1, 0), e) * step + step - 1, j)
    )
    return pl.pallas_call(
        functools.partial(backward_kernel, count, seq),
        grid_spec=pltpu.PrefetchScalarGridSpec(
            num_scalar_prefetch=1,
            grid=(chunks,),
            in_specs=[
                blk(width, 0), blk(width, 1), halo(width, 1), blk(256, 0), halo(256, 0), blk(128, 2),
                blk(width), blk(width), pl.BlockSpec((1, 128, width), lambda g, e: (last - g, 0, 0)), blk(256),
                fixed((5, width)), fixed((5, 256)), fixed((2, 128)), fixed((2, width)),
            ],
            out_specs=[blk(2 * width), blk(256), blk(128)],
            scratch_shapes=[
                pltpu.VMEM((128, width), F32), pltpu.VMEM((HALO, width), F32), pltpu.VMEM((HALO, 256), F32),
                pltpu.VMEM((8, 128), F32),
            ],
        ),
        out_shape=[
            jax.ShapeDtypeStruct((seq, 2 * width), BF16),
            jax.ShapeDtypeStruct((seq, 256), BF16),
            jax.ShapeDtypeStruct((seq, 128), BF16),
        ],
        compiler_params=pltpu.CompilerParams(dimension_semantics=("arbitrary",)),
        cost_estimate=pl.CostEstimate(
            flops=seq * width * 3000, bytes_accessed=seq * width * 24, transcendentals=seq * width * 8
        ),
        name="mixer_backward",
    )(ends, zx, zx, zx, small, small, small, gm, y, states, rk, taps, bctaps, heads, chans)


EPS = 1e-05
ROW_LEN = 1024


def dot(a, b, dims=NN):
    return lax.dot_general(a, b, dims, preferred_element_type=F32)


def row_places(own_row, core, flipped):
    shift = core * (ROW_LEN // 2) if flipped else 0
    return jnp.remainder(jnp.arange(ROW_LEN, dtype=jnp.int32) + shift, ROW_LEN)


def row_select(ends, ids, places, columns):
    segment = jnp.sum((places[:, None] >= ends[None, :]).astype(jnp.int32), axis=1)
    member = segment[:, None] == jnp.arange(ends.shape[0], dtype=jnp.int32)[None, :]
    adapter = jnp.sum(jnp.where(member, ids[None, :], 0), axis=1)
    return (adapter[:, None] == columns[None, :]).astype(F32)


def flip(v):
    half = v.shape[-1] // 2
    return jnp.concatenate([v[..., half:], v[..., :half]], axis=-1)


class PairedLinks:
    flipped = True

    def __init__(self):
        me = lax.axis_index("tensor")
        self.own_row, self.core = me // 2, me % 2
        self.across = [(i, i ^ 2) for i in range(4)]
        self.beside = [(i, i ^ 1) for i in range(4)]

    def far(self, v):
        return lax.ppermute(v, "tensor", self.across)

    def near(self, v):
        return lax.ppermute(v, "tensor", self.beside)

    def gather(self, v):
        own = jnp.concatenate([v, self.near(v)], axis=0)
        came = self.far(v)
        return own, jnp.concatenate([came, self.near(came)], axis=0)

    def sum_stats(self, own, other):
        both = jnp.stack([own, other])
        both = both + flip(self.near(both))
        came = self.far(both)
        return both[0] + came[1], both[1] + came[0]

    def reduce_other(self, project):
        half = ROW_LEN // 2
        second = self.near(project(half, ROW_LEN).astype(BF16))
        first = project(0, half)
        return self.far((first + second.astype(F32)).astype(BF16))

    def reduce_own(self, project, came):
        half = ROW_LEN // 2
        second = self.near(project(half, ROW_LEN).astype(BF16))
        return project(0, half) + second.astype(F32) + came.astype(F32)

    def mine(self, own_stat):
        return own_stat[: ROW_LEN // 2]


class GroupLinks:
    flipped = False

    def __init__(self, parts, rows):
        me = lax.axis_index("tensor")
        per_row = parts // rows
        self.own_row, self.core = me // per_row, me % per_row
        self.per_row = per_row

    def gather(self, v):
        whole = lax.all_gather(v, "tensor", axis=0, tiled=True).reshape(2, ROW_LEN, v.shape[1])
        return (
            lax.dynamic_index_in_dim(whole, self.own_row, 0, False),
            lax.dynamic_index_in_dim(whole, 1 - self.own_row, 0, False),
        )

    def sum_stats(self, own, other):
        first = jnp.where(self.own_row == 0, own, other)
        second = jnp.where(self.own_row == 0, other, own)
        total = lax.psum(jnp.stack([first, second]), "tensor")
        return (
            lax.dynamic_index_in_dim(total, self.own_row, 0, False),
            lax.dynamic_index_in_dim(total, 1 - self.own_row, 0, False),
        )

    def reduce_other(self, project):
        return project(0, ROW_LEN).astype(BF16)

    def reduce_own(self, project, other):
        own = project(0, ROW_LEN).astype(BF16)
        first = jnp.where(self.own_row == 0, own, other)
        second = jnp.where(self.own_row == 0, other, own)
        whole = jnp.concatenate([first, second], axis=0)
        return lax.psum_scatter(whole, "tensor", scatter_dimension=0, tiled=True).astype(F32)

    def mine(self, own_stat):
        size = ROW_LEN // self.per_row
        return lax.dynamic_slice_in_dim(own_stat, self.core * size, size, 0)


def on_device(
    tokens, cotangent, lengths, ids, deal, norm_gain, zx_weight, state_weight, step_weight,
    conv_taps, state_taps, head_values, gated_gain, out_weight, in_down, in_up, out_down, out_up,
):
    tok_dev, model = tokens.shape
    parts = lax.axis_size("tensor")
    rows = tok_dev * parts // ROW_LEN
    assert rows == 2
    links = PairedLinks() if parts == 4 else GroupLinks(parts, rows)
    adapters, rank = in_down.shape[1:]
    reduced = adapters * rank
    width = zx_weight.shape[2]
    inner = width * parts
    heads_here = width // HEAD
    in_down = in_down.reshape(model, reduced)
    in_up = in_up.reshape(reduced, 2 * width)
    out_down = out_down.reshape(width, reduced)
    out_up = out_up.reshape(reduced, model)
    zx_weight = zx_weight.reshape(model, 2 * width)
    pad = lambda v: jnp.pad(v, ((0, 0), (0, 128 - heads_here)))
    small_weight = jnp.concatenate([state_weight, pad(step_weight), in_down], axis=1)
    heads = jnp.concatenate([pad(head_values[0:1]), pad(-jnp.exp(head_values[1:2]))], axis=0)
    chans = jnp.stack([jnp.repeat(head_values[2], HEAD), gated_gain])
    columns = jnp.arange(reduced, dtype=jnp.int32) // rank

    places = row_places(links.own_row, links.core, links.flipped)
    turn = (links.core if links.flipped else 0) * jnp.ones((1,), jnp.int32)
    base = lax.axis_index("dp") * rows
    row_data = []
    for which in (links.own_row, 1 - links.own_row):
        packed = lax.dynamic_index_in_dim(deal, base + which, 0, False)
        ends = jnp.cumsum(lax.dynamic_index_in_dim(lengths, packed, 0, False))
        row_ids = lax.dynamic_index_in_dim(ids, packed, 0, False)
        select = row_select(ends, row_ids, places, columns)
        row_data.append((jnp.concatenate([ends, turn]).astype(jnp.int32), select))

    residual = tokens.astype(F32)
    inv_rms = lax.rsqrt(jnp.mean(residual * residual, axis=1, keepdims=True) + EPS)
    normed = links.gather((residual * inv_rms * norm_gain).astype(BF16))
    cots = links.gather(cotangent)

    def forward(row):
        ends, select = row_data[row]
        nb = normed[row]
        small = dot(nb, small_weight)
        lora = (small[:, 384:] * select).astype(BF16)
        zx = dot(nb, zx_weight) + dot(lora, in_up)
        y, gained, squares, states = mixer_forward(ends, zx, small, conv_taps, state_taps, heads, chans)
        return small, lora, zx, y, gained, squares, states

    def cotangents(row):
        low = (dot(cots[row], out_up, NT) * row_data[row][1]).astype(BF16)
        return low, dot(cots[row], out_weight, NT) + dot(low, out_down, NT)

    def project_out(row, gained):
        def part(first, last):
            piece = gained[first:last]
            low = (dot(piece, out_down) * row_data[row][1][first:last]).astype(BF16)
            return dot(piece, out_weight) + dot(low, out_up)

        return part

    fw = [forward(0), forward(1)]
    back = [cotangents(0), cotangents(1)]
    crosses = [jnp.sum(back[r][1] * fw[r][4].astype(F32), axis=1) for r in range(2)]
    stats = [jnp.stack([fw[r][5][0], crosses[r]]) for r in range(2)]
    stats = links.sum_stats(stats[0], stats[1])
    came = links.reduce_other(project_out(1, fw[1][4]))
    out_sum = links.reduce_own(project_out(0, fw[0][4]), came)
    inv, rks = [], []
    for r in range(2):
        scale = lax.rsqrt(stats[r][0] / inner + EPS)
        kappa = scale * scale * (stats[r][1] / inner)
        inv.append(scale)
        rks.append(
            jnp.concatenate(
                [jnp.broadcast_to(scale[:, None], (ROW_LEN, 128)), jnp.broadcast_to(kappa[:, None], (ROW_LEN, 128))],
                axis=1,
            )
        )
    output = (residual + links.mine(inv[0])[:, None] * out_sum).astype(BF16)

    grads = [None, None]
    out_grads = [None, None]
    for r in (1, 0):
        low, gm = back[r]
        gained = fw[r][4]
        select = row_data[r][1]
        scaled_low = (low.astype(F32) * inv[r][:, None]).astype(BF16)
        lora_back = (dot(gained, out_down) * select * inv[r][:, None]).astype(BF16)
        out_grads[r] = (
            lax.dot_general(gained, scaled_low, TN, preferred_element_type=F32),
            lax.dot_general(lora_back, cots[r], TN, preferred_element_type=F32),
        )
    down_total, up_total = [a + b for a, b in zip(*out_grads)]

    in_grads = [None, None]
    for r in (1, 0):
        ends, select = row_data[r]
        small, lora, zx, y, gained, _, states = fw[r]
        dzx, dbc, ddt = mixer_backward(
            ends, zx, small, back[r][1], y, states, rks[r], conv_taps, state_taps, heads, chans
        )
        mid = (dot(dzx, in_up, NT) * select).astype(BF16)
        in_grads[r] = (
            lax.dot_general(lora, dzx, TN, preferred_element_type=F32),
            lax.dot_general(normed[r], mid, TN, preferred_element_type=F32),
        )
        dsmall = jnp.concatenate([dbc, ddt, mid], axis=1)

        def part(first, last, dzx=dzx, dsmall=dsmall):
            return dot(dzx[first:last], zx_weight, NT) + dot(dsmall[first:last], small_weight, NT)

        grads[r] = part
        if r == 1:
            came = links.reduce_other(part)
    grad_normed = links.reduce_own(grads[0], came)
    in_up_total, in_down_total = [a + b for a, b in zip(*in_grads)]

    scaled = grad_normed * norm_gain
    grad_tokens = (
        cotangent.astype(F32)
        + inv_rms * scaled
        - residual * inv_rms**3 * (jnp.sum(scaled * residual, axis=1, keepdims=True) / model)
    )
    out_up_sum = lax.psum(up_total.astype(BF16), ("dp", "tensor")).astype(F32)
    out_down_sum = lax.psum(down_total.astype(BF16), "dp").astype(F32)
    in_down_sum = lax.psum(in_down_total.astype(BF16), ("dp", "tensor")).astype(F32)
    in_up_sum = lax.psum(in_up_total.astype(BF16), "dp").astype(F32)
    return (
        output,
        grad_tokens,
        in_down_sum.reshape(model, adapters, rank),
        in_up_sum.reshape(adapters, rank, 2, width),
        out_down_sum.reshape(width, adapters, rank),
        out_up_sum.reshape(adapters, rank, model),
    )


def solution(mesh):
    return jax.shard_map(
        on_device,
        mesh=mesh,
        in_specs=(
            P(("dp", "tensor"), None), P(("dp", "tensor"), None), P(), P(), P(), P(),
            P(None, None, "tensor"), P(), P(None, "tensor"), P(None, "tensor"), P(), P(None, "tensor"),
            P("tensor"), P("tensor", None), P(), P(None, None, None, "tensor"), P("tensor", None, None), P(),
        ),
        out_specs=(
            P(("dp", "tensor"), None), P(("dp", "tensor"), None), P(),
            P(None, None, None, "tensor"), P("tensor", None, None), P(),
        ),
        check_vma=False,
    )
```

```python
import functools

import jax
import jax.numpy as jnp
from jax import lax
from jax.experimental import pallas as pl
from jax.experimental.pallas import tpu as pltpu
from jax.sharding import PartitionSpec as P

F32, BF16 = jnp.float32, jnp.bfloat16
L = 128
HEAD = 64
HALO = 8
NN = (((1,), (0,)), ((), ()))
NT = (((1,), (1,)), ((), ()))
TN = (((0,), (0,)), ((), ()))


def mm(a, b, dims=NN):
    return lax.dot_general(a, b, dims, preferred_element_type=F32)


def split2(v):
    hi = v.astype(BF16)
    return hi, (v - hi.astype(F32)).astype(BF16)


def split3(v):
    hi = v.astype(BF16)
    rest = v - hi.astype(F32)
    mid = rest.astype(BF16)
    return hi, mid, (rest - mid.astype(F32)).astype(BF16)


def sigmoid(v):
    return 0.5 * jnp.tanh(0.5 * v) + 0.5


def starts_of(pos, ends, count):
    start = jnp.zeros_like(pos)
    for k in range(count - 1):
        start = jnp.where(pos >= ends[k], jnp.maximum(start, ends[k]), start)
    return start


def scalar_start(pos, ends, count):
    start = jnp.int32(0)
    for k in range(count - 1):
        start = jnp.where(pos >= ends[k], jnp.maximum(start, ends[k]), start)
    return start


def chunk_geometry(t0, ends, count):
    rows = t0 + lax.broadcasted_iota(jnp.int32, (L, L), 0)
    cols = t0 + lax.broadcasted_iota(jnp.int32, (L, L), 1)
    row_start = starts_of(rows, ends, count)
    col_start = starts_of(cols, ends, count)
    last_start = scalar_start(t0 + (L - 1), ends, count)
    return rows, cols, row_start, col_start, last_start


def conv_tile(ext, taps, within):
    total = ext[HALO:] * taps[3:4] + taps[4:5]
    for lag in range(1, 4):
        moved = pltpu.roll(ext, lag, 0)[HALO:]
        total = total + jnp.where(within >= lag, moved, 0.0) * taps[3 - lag : 4 - lag]
    return total


def conv_back(ext, taps, ok):
    size = ext.shape[0]
    total = ext[:L] * taps[3:4]
    for lag in range(1, 4):
        moved = pltpu.roll(ext, size - lag, 0)[:L]
        total = total + jnp.where(ok[lag - 1], moved, 0.0) * taps[3 - lag : 4 - lag]
    return total


def step_terms(dt_raw, bias, rate, low_mask):
    raw = dt_raw + bias
    dt = jnp.maximum(raw, 0.0) + jnp.log1p(jnp.exp(-jnp.abs(raw)))
    decay = dt * rate
    cum = sum(mm(low_mask, part) for part in split3(decay))
    return raw, dt, cum


def lane_pair(low, value, h):
    first = jnp.broadcast_to(value[:, h : h + 1], (L, 128))
    second = jnp.broadcast_to(value[:, h + 1 : h + 2], (L, 128))
    return first, second, jnp.where(low, first, second)


def forward_kernel(
    count, ends, z_ref, x_ref, bc_ref, dt_ref, taps_ref, bct_ref, head_ref, chan_ref,
    y_ref, g_ref, sum_ref, st_ref, state, xprev, bcprev,
):
    c = pl.program_id(0)
    pairs = x_ref.shape[1] // 128

    @pl.when(c == 0)
    def _():
        state[...] = jnp.zeros_like(state)
        xprev[...] = jnp.zeros_like(xprev)
        bcprev[...] = jnp.zeros_like(bcprev)

    t0 = c * L
    rows, cols, row_start, col_start, last_start = chunk_geometry(t0, ends, count)
    within = rows - row_start
    mask = (row_start == col_start) & (cols <= rows)
    low_mask = jnp.where(mask, 1.0, 0.0).astype(BF16)
    contin = row_start < t0
    tail = row_start == last_start
    keep = jnp.where(last_start < t0, 1.0, 0.0).astype(F32)
    low = lax.broadcasted_iota(jnp.int32, (L, 128), 1) < HEAD

    bc_halves = []
    for half in range(2):
        cut = slice(half * 128, half * 128 + 128)
        ext = jnp.concatenate([bcprev[:, cut], bc_ref[:, cut]], axis=0)
        pre = conv_tile(ext, bct_ref[:, cut], within)
        bc_halves.append((pre * sigmoid(pre)))
    b_mat, c_mat = bc_halves
    b_low, c_low = b_mat.astype(BF16), c_mat.astype(BF16)
    b_turn = b_mat.T.astype(BF16)
    scores = jnp.where(mask, mm(c_low, b_low, NT), 0.0)

    _, dt, cum = step_terms(dt_ref[...], head_ref[0:1], head_ref[1:2], low_mask)
    cum_turn = cum.T

    squares = jnp.zeros((L, 128), F32)
    for p in range(pairs):
        cut = slice(p * 128, p * 128 + 128)
        ext = jnp.concatenate([xprev[:, cut], x_ref[:, cut]], axis=0)
        pre = conv_tile(ext, taps_ref[:, cut], within)
        xc = pre * sigmoid(pre)
        c0, c1, c_both = lane_pair(low, cum, 2 * p)
        _, _, dt_both = lane_pair(low, dt, 2 * p)
        xt = xc * dt_both
        xb = xt.astype(BF16)
        zero = jnp.zeros_like(xb)
        x2 = jnp.concatenate([jnp.where(low, xb, zero), jnp.where(low, zero, xb)], axis=0)
        g0 = (scores * jnp.exp(jnp.minimum(c0 - cum_turn[2 * p : 2 * p + 1], 0.0))).astype(BF16)
        g1 = (scores * jnp.exp(jnp.minimum(c1 - cum_turn[2 * p + 1 : 2 * p + 2], 0.0))).astype(BF16)
        inside = mm(jnp.concatenate([g0, g1], axis=1), x2)
        old = state[:, cut]
        old_low = old.astype(BF16)
        st_ref[0, :, cut] = old_low
        carried = jnp.where(contin, jnp.exp(c_both), 0.0)
        y = inside + mm(c_low, old_low) * carried
        y_ref[:, cut] = y
        c_last = c_both[L - 1 :, :]
        tail_w = jnp.where(tail, jnp.exp(c_last - c_both), 0.0)
        state[:, cut] = (keep * jnp.exp(c_last)) * old + mm(b_turn, (xt * tail_w).astype(BF16))
        z = z_ref[:, cut]
        gated = (y + chan_ref[0:1, cut] * xc) * (z * sigmoid(z))
        gained = gated * chan_ref[1:2, cut]
        g_ref[:, cut] = gained.astype(BF16)
        squares = squares + gated * gated
    ones = jnp.ones((8, 128), BF16)
    sq_row = sum(mm(ones, part, NT) for part in split3(squares))
    sum_ref[...] = sq_row
    xprev[...] = x_ref[L - HALO :, :]
    bcprev[...] = bc_ref[L - HALO :, :]


def backward_kernel(
    count, seq, ends, z_ref, x_ref, xh_ref, bc_ref, bch_ref, dt_ref, gm_ref, y_ref, st_ref, rk_ref,
    taps_ref, bct_ref, head_ref, chan_ref,
    dzx_ref, dbc_ref, ddt_ref, dstate, dnext, dbnext, ends_row,
):
    g = pl.program_id(0)
    c = pl.num_programs(0) - 1 - g
    width = x_ref.shape[1]
    pairs = width // 128

    @pl.when(g == 0)
    def _():
        dstate[...] = jnp.zeros_like(dstate)
        dnext[...] = jnp.zeros_like(dnext)
        dbnext[...] = jnp.zeros_like(dbnext)
        ends_row[...] = jnp.zeros_like(ends_row)

    t0 = c * L
    rows, cols, row_start, col_start, last_start = chunk_geometry(t0, ends, count)
    within = rows - row_start
    same = row_start == col_start
    low_mask = jnp.where(same & (cols <= rows), 1.0, 0.0).astype(BF16)
    up = same & (rows <= cols)
    up_mask = jnp.where(up, 1.0, 0.0).astype(BF16)
    contin = row_start < t0
    tail = row_start == last_start
    keep = jnp.where(last_start < t0, 1.0, 0.0).astype(F32)
    lane = lax.broadcasted_iota(jnp.int32, (L, 128), 1)
    sub = lax.broadcasted_iota(jnp.int32, (L, 128), 0)
    low = lane < HEAD
    ok = [
        (rows + lag < seq) & (starts_of(rows + lag, ends, count) <= rows) for lag in range(1, 4)
    ]

    parts = []
    for half in range(2):
        cut = slice(half * 128, half * 128 + 128)
        ext = jnp.concatenate([bch_ref[:, cut], bc_ref[:, cut]], axis=0)
        pre = conv_tile(ext, bct_ref[:, cut], within)
        sg = sigmoid(pre)
        act = pre * sg
        parts.append((act, sg + act * (1.0 - sg)))
    (b_mat, b_slope), (c_mat, c_slope) = parts
    b_low, c_low = b_mat.astype(BF16), c_mat.astype(BF16)
    c_turn = c_mat.T.astype(BF16)
    scores = jnp.where(up, mm(b_low, c_low, NT), 0.0)

    raw, dt, cum = step_terms(dt_ref[...], head_ref[0:1], head_ref[1:2], low_mask)
    cum_turn = cum.T
    inv, kappa = rk_ref[:, :128], rk_ref[:, 128:]

    d_scores = jnp.zeros((L, L), F32)
    d_b = jnp.zeros((L, 128), F32)
    d_c = jnp.zeros((L, 128), F32)
    d_cum = jnp.zeros((L, 128), F32)
    d_dt = jnp.zeros((L, 128), F32)
    d_end = jnp.zeros((8, 128), F32)
    for p in range(pairs):
        cut = slice(p * 128, p * 128 + 128)
        pick = jnp.where(lane == 2 * p + jnp.where(sub >= HEAD, 1, 0), 1.0, 0.0).astype(BF16)
        ext = jnp.concatenate([xh_ref[:, cut], x_ref[:, cut]], axis=0)
        taps = taps_ref[:, cut]
        pre = conv_tile(ext, taps, within)
        sg = sigmoid(pre)
        xc = pre * sg
        skip = chan_ref[0:1, cut]
        z = z_ref[:, cut]
        sz = sigmoid(z)
        sil = z * sz
        y = y_ref[:, cut]
        yt = y + skip * xc
        gg = inv * (gm_ref[:, cut] * chan_ref[1:2, cut] - kappa * (yt * sil))
        dzx_ref[:, cut] = (gg * yt * (sz + sil * (1.0 - sz))).astype(BF16)
        dyt = gg * sil
        dyb = dyt.astype(BF16)
        zero = jnp.zeros_like(dyb)
        dy2 = jnp.concatenate([jnp.where(low, dyb, zero), jnp.where(low, zero, dyb)], axis=0)
        c0, c1, c_both = lane_pair(low, cum, 2 * p)
        _, _, dt_both = lane_pair(low, dt, 2 * p)
        xt = xc * dt_both
        xb = xt.astype(BF16)
        dg = mm(xb, dy2, NT)
        w0 = jnp.exp(jnp.minimum(cum_turn[2 * p : 2 * p + 1] - c0, 0.0))
        w1 = jnp.exp(jnp.minimum(cum_turn[2 * p + 1 : 2 * p + 2] - c1, 0.0))
        d_scores = d_scores + dg[:, :L] * w0 + dg[:, L:] * w1
        gt = jnp.concatenate([(scores * w0).astype(BF16), (scores * w1).astype(BF16)], axis=1)
        carried = jnp.where(contin, jnp.exp(c_both), 0.0)
        c_last = c_both[L - 1 :, :]
        tail_w = jnp.where(tail, jnp.exp(c_last - c_both), 0.0)
        ds = dstate[:, cut]
        ds_low = ds.astype(BF16)
        dxt = mm(gt, dy2) + mm(b_low, ds_low) * tail_w
        dyc = (dyt * carried).astype(BF16)
        st = st_ref[0, :, cut]
        d_c = d_c + mm(dyc, st, NT)
        d_b = d_b + mm((xt * tail_w).astype(BF16), ds_low, NT)
        ds_new = (keep * jnp.exp(c_last)) * ds + mm(c_turn, dyc)
        dstate[:, cut] = ds_new
        both = jnp.sum(ds_new * st.astype(F32), axis=0, keepdims=True)
        both = jnp.broadcast_to(both, (8, 128))
        d_end = d_end + sum(mm(part, pick) for part in split2(both))
        v = dyb.astype(F32) * y - xb.astype(F32) * dxt
        d_cum = d_cum + sum(mm(part, pick) for part in split2(v))
        d_dt = d_dt + sum(mm(part, pick) for part in split2(dxt * xc))
        dpre = (skip * dyt + dt_both * dxt) * (sg + xc * (1.0 - sg))
        ext = jnp.concatenate([dpre, dnext[:, cut]], axis=0)
        dzx_ref[:, slice(width + p * 128, width + p * 128 + 128)] = conv_back(ext, taps, ok).astype(BF16)
        dnext[:, cut] = dpre[:HALO]

    d_scores = jnp.where(up, d_scores, 0.0)
    d_b = d_b + mm(d_scores.astype(BF16), c_low)
    d_c = d_c + mm(d_scores.T.astype(BF16), b_low)
    for half, (grad, slope) in enumerate(((d_b, b_slope), (d_c, c_slope))):
        cut = slice(half * 128, half * 128 + 128)
        dpre = grad * slope
        ext = jnp.concatenate([dpre, dbnext[:, cut]], axis=0)
        dbc_ref[:, cut] = conv_back(ext, bct_ref[:, cut], ok).astype(BF16)
        dbnext[:, cut] = dpre[:HALO]
    d_cum = d_cum + jnp.where(sub == L - 1, ends_row[0:1, :], 0.0)
    ends_row[...] = d_end
    d_decay = sum(mm(up_mask, part) for part in split3(d_cum))
    ddt_ref[...] = ((d_dt + head_ref[1:2] * d_decay) * sigmoid(raw)).astype(BF16)


def mixer_forward(ends, zx, small, taps, bctaps, heads, chans):
    seq, width = zx.shape[0], zx.shape[1] // 2
    count = ends.shape[0] - 1
    chunks = seq // L
    place = lambda c, e: lax.rem(c + e[count] * (chunks // 2), chunks)
    fixed = lambda shape: pl.BlockSpec(shape, lambda c, e: (0,) * len(shape))
    blk = lambda w, j=0: pl.BlockSpec((L, w), lambda c, e: (place(c, e), j))
    return pl.pallas_call(
        functools.partial(forward_kernel, count),
        grid_spec=pltpu.PrefetchScalarGridSpec(
            num_scalar_prefetch=1,
            grid=(chunks,),
            in_specs=[
                blk(width, 0), blk(width, 1), blk(256, 0), blk(128, 2),
                fixed((5, width)), fixed((5, 256)), fixed((2, 128)), fixed((2, width)),
            ],
            out_specs=[
                blk(width), blk(width), pl.BlockSpec((8, L), lambda c, e: (0, place(c, e))),
                pl.BlockSpec((1, 128, width), lambda c, e: (c, 0, 0)),
            ],
            scratch_shapes=[
                pltpu.VMEM((128, width), F32), pltpu.VMEM((HALO, width), F32), pltpu.VMEM((HALO, 256), F32),
            ],
        ),
        out_shape=[
            jax.ShapeDtypeStruct((seq, width), F32),
            jax.ShapeDtypeStruct((seq, width), BF16),
            jax.ShapeDtypeStruct((8, seq), F32),
            jax.ShapeDtypeStruct((chunks, 128, width), BF16),
        ],
        compiler_params=pltpu.CompilerParams(dimension_semantics=("arbitrary",)),
        cost_estimate=pl.CostEstimate(
            flops=seq * width * 1200, bytes_accessed=seq * width * 16, transcendentals=seq * width * 6
        ),
        name="mixer_forward",
    )(ends, zx, zx, small, small, taps, bctaps, heads, chans)


def mixer_backward(ends, zx, small, gm, y, states, rk, taps, bctaps, heads, chans):
    seq, width = gm.shape
    count = ends.shape[0] - 1
    chunks = seq // L
    last = chunks - 1
    step = L // HALO
    place = lambda c, e: lax.rem(c + e[count] * (chunks // 2), chunks)
    fixed = lambda shape: pl.BlockSpec(shape, lambda g, e: (0,) * len(shape))
    blk = lambda w, j=0: pl.BlockSpec((L, w), lambda g, e: (place(last - g, e), j))
    halo = lambda w, j=0: pl.BlockSpec(
        (HALO, w), lambda g, e: (place(jnp.maximum(last - g - 1, 0), e) * step + step - 1, j)
    )
    return pl.pallas_call(
        functools.partial(backward_kernel, count, seq),
        grid_spec=pltpu.PrefetchScalarGridSpec(
            num_scalar_prefetch=1,
            grid=(chunks,),
            in_specs=[
                blk(width, 0), blk(width, 1), halo(width, 1), blk(256, 0), halo(256, 0), blk(128, 2),
                blk(width), blk(width), pl.BlockSpec((1, 128, width), lambda g, e: (last - g, 0, 0)), blk(256),
                fixed((5, width)), fixed((5, 256)), fixed((2, 128)), fixed((2, width)),
            ],
            out_specs=[blk(2 * width), blk(256), blk(128)],
            scratch_shapes=[
                pltpu.VMEM((128, width), F32), pltpu.VMEM((HALO, width), F32), pltpu.VMEM((HALO, 256), F32),
                pltpu.VMEM((8, 128), F32),
            ],
        ),
        out_shape=[
            jax.ShapeDtypeStruct((seq, 2 * width), BF16),
            jax.ShapeDtypeStruct((seq, 256), BF16),
            jax.ShapeDtypeStruct((seq, 128), BF16),
        ],
        compiler_params=pltpu.CompilerParams(dimension_semantics=("arbitrary",)),
        cost_estimate=pl.CostEstimate(
            flops=seq * width * 3000, bytes_accessed=seq * width * 24, transcendentals=seq * width * 8
        ),
        name="mixer_backward",
    )(ends, zx, zx, zx, small, small, small, gm, y, states, rk, taps, bctaps, heads, chans)


EPS = 1e-05
ROW_LEN = 1024


def dot(a, b, dims=NN):
    return lax.dot_general(a, b, dims, preferred_element_type=F32)


def row_places(own_row, core, flipped):
    shift = core * (ROW_LEN // 2) if flipped else 0
    return jnp.remainder(jnp.arange(ROW_LEN, dtype=jnp.int32) + shift, ROW_LEN)


def row_select(ends, ids, places, columns):
    segment = jnp.sum((places[:, None] >= ends[None, :]).astype(jnp.int32), axis=1)
    member = segment[:, None] == jnp.arange(ends.shape[0], dtype=jnp.int32)[None, :]
    adapter = jnp.sum(jnp.where(member, ids[None, :], 0), axis=1)
    return (adapter[:, None] == columns[None, :]).astype(F32)


def flip(v):
    half = v.shape[-1] // 2
    return jnp.concatenate([v[..., half:], v[..., :half]], axis=-1)


class PairedLinks:
    flipped = True

    def __init__(self):
        me = lax.axis_index("tensor")
        self.own_row, self.core = me // 2, me % 2
        self.across = [(i, i ^ 2) for i in range(4)]
        self.beside = [(i, i ^ 1) for i in range(4)]

    def far(self, v):
        return lax.ppermute(v, "tensor", self.across)

    def near(self, v):
        return lax.ppermute(v, "tensor", self.beside)

    def gather_own(self, v):
        return jnp.concatenate([v, self.near(v)], axis=0)

    def send_other(self, v):
        return self.far(v)

    def gather_other(self, came):
        return jnp.concatenate([came, self.near(came)], axis=0)

    def sum_stats(self, own, other):
        both = jnp.stack([own, other])
        both = both + flip(self.near(both))
        came = self.far(both)
        return both[0] + came[1], both[1] + came[0]

    def reduce_near(self, whole):
        half = ROW_LEN // 2
        second = self.near(whole[half:])
        return whole[:half].astype(F32) + second.astype(F32)

    def reduce_other(self, whole):
        sent = self.reduce_near(whole).astype(BF16)
        return sent, self.far(sent)

    def reduce_own(self, whole, came):
        return self.reduce_near(whole) + came.astype(F32)

    def mine(self, own_stat):
        return own_stat[: ROW_LEN // 2]


class GroupLinks:
    flipped = False

    def __init__(self, parts, rows):
        me = lax.axis_index("tensor")
        per_row = parts // rows
        self.own_row, self.core = me // per_row, me % per_row
        self.per_row = per_row

    def gather_row(self, v, row):
        whole = lax.all_gather(v, "tensor", axis=0, tiled=True).reshape(2, ROW_LEN, v.shape[1])
        return lax.dynamic_index_in_dim(whole, row, 0, False)

    def gather_own(self, v):
        return self.gather_row(v, self.own_row)

    def send_other(self, v):
        return v

    def gather_other(self, v):
        return self.gather_row(v, 1 - self.own_row)

    def sum_stats(self, own, other):
        first = jnp.where(self.own_row == 0, own, other)
        second = jnp.where(self.own_row == 0, other, own)
        total = lax.psum(jnp.stack([first, second]), "tensor")
        return (
            lax.dynamic_index_in_dim(total, self.own_row, 0, False),
            lax.dynamic_index_in_dim(total, 1 - self.own_row, 0, False),
        )

    def reduce_other(self, whole):
        return whole, whole

    def reduce_own(self, own, other):
        first = jnp.where(self.own_row == 0, own, other)
        second = jnp.where(self.own_row == 0, other, own)
        whole = jnp.concatenate([first, second], axis=0)
        return lax.psum_scatter(whole, "tensor", scatter_dimension=0, tiled=True).astype(F32)

    def mine(self, own_stat):
        size = ROW_LEN // self.per_row
        return lax.dynamic_slice_in_dim(own_stat, self.core * size, size, 0)


def after(v, *done):
    return lax.optimization_barrier((v,) + done)[0]


def exchange_steps(axis):
    size = lax.axis_size(axis)
    assert size & (size - 1) == 0
    steps, mask = [], 1
    while mask < size:
        bit = (lax.axis_index(axis) // mask) % 2
        steps.append((axis, bit, [(i, i ^ mask) for i in range(size)]))
        mask *= 2
    return steps


def half_of(v, which):
    size = v.shape[0] // 2
    return lax.dynamic_slice_in_dim(v, which * size, size, 0)


def scatter_sum(arrays, step):
    axis, bit, pairs = step
    sent = jnp.concatenate([half_of(v, 1 - bit) for v in arrays], axis=0).astype(BF16)
    came = lax.ppermute(sent, axis, pairs).astype(F32)
    sums, first = [], 0
    for v in arrays:
        size = v.shape[0] // 2
        sums.append(half_of(v, bit) + came[first : first + size])
        first += size
    return sums


def gather_halves(arrays, step):
    axis, bit, pairs = step
    came = lax.ppermute(jnp.concatenate(arrays, axis=0), axis, pairs)
    wholes, first = [], 0
    for v in arrays:
        other = came[first : first + v.shape[0]]
        first += v.shape[0]
        wholes.append(
            jnp.concatenate([jnp.where(bit == 0, v, other), jnp.where(bit == 0, other, v)], axis=0)
        )
    return wholes


class FactorSum:
    def __init__(self, shared, split):
        self.near, self.far = exchange_steps("tensor"), exchange_steps("dp")
        self.arrays, self.split, self.done = [shared], split, 0

    def hop(self):
        near, far = len(self.near), len(self.far)
        at, total = self.done, 2 * (near + far)
        if at == total:
            return
        if at == near:
            self.arrays = self.arrays + [self.split]
        if at == near + far:
            self.arrays = [v.astype(BF16) for v in self.arrays]
        steps = self.near + self.far
        if at < near + far:
            self.arrays = scatter_sum(self.arrays, steps[at])
        else:
            self.arrays = gather_halves(self.arrays, steps[total - 1 - at])
        self.done += 1
        if self.done == near + 2 * far:
            self.split = self.arrays[1]
            self.arrays = self.arrays[:1]

    def cover(self, v):
        v, *self.arrays = lax.optimization_barrier((v, *self.arrays))
        self.hop()
        return v

    def finish(self):
        while self.done < 2 * (len(self.near) + len(self.far)):
            self.hop()
        return self.arrays[0].astype(F32), self.split.astype(F32)


def on_device(
    tokens, cotangent, lengths, ids, deal, norm_gain, zx_weight, state_weight, step_weight,
    conv_taps, state_taps, head_values, gated_gain, out_weight, in_down, in_up, out_down, out_up,
):
    tok_dev, model = tokens.shape
    parts = lax.axis_size("tensor")
    rows = tok_dev * parts // ROW_LEN
    assert rows == 2
    links = PairedLinks() if parts == 4 else GroupLinks(parts, rows)
    adapters, rank = in_down.shape[1:]
    reduced = adapters * rank
    width = zx_weight.shape[2]
    inner = width * parts
    heads_here = width // HEAD
    in_down = in_down.reshape(model, reduced)
    in_up = in_up.reshape(reduced, 2 * width)
    out_down = out_down.reshape(width, reduced)
    out_up = out_up.reshape(reduced, model)
    zx_weight = zx_weight.reshape(model, 2 * width)
    pad = lambda v: jnp.pad(v, ((0, 0), (0, 128 - heads_here)))
    small_weight = jnp.concatenate([state_weight, pad(step_weight), in_down], axis=1)
    heads = jnp.concatenate([pad(head_values[0:1]), pad(-jnp.exp(head_values[1:2]))], axis=0)
    chans = jnp.stack([jnp.repeat(head_values[2], HEAD), gated_gain])
    columns = jnp.arange(reduced, dtype=jnp.int32) // rank

    places = row_places(links.own_row, links.core, links.flipped)
    turn = (links.core if links.flipped else 0) * jnp.ones((1,), jnp.int32)
    base = lax.axis_index("dp") * rows
    row_data = []
    for which in (links.own_row, 1 - links.own_row):
        packed = lax.dynamic_index_in_dim(deal, base + which, 0, False)
        ends = jnp.cumsum(lax.dynamic_index_in_dim(lengths, packed, 0, False))
        row_ids = lax.dynamic_index_in_dim(ids, packed, 0, False)
        select = row_select(ends, row_ids, places, columns)
        row_data.append((jnp.concatenate([ends, turn]).astype(jnp.int32), select))

    residual = tokens.astype(F32)
    inv_rms = lax.rsqrt(jnp.mean(residual * residual, axis=1, keepdims=True) + EPS)
    normed_here = (residual * inv_rms * norm_gain).astype(BF16)
    normed = [links.gather_own(normed_here), links.gather_other(links.send_other(normed_here))]
    cots = [links.gather_own(cotangent), None]

    def forward(row, nb):
        ends, select = row_data[row]
        small = dot(nb, small_weight)
        lora = (small[:, 384:] * select).astype(BF16)
        zx = dot(nb, zx_weight) + dot(lora, in_up)
        y, gained, squares, states = mixer_forward(ends, zx, small, conv_taps, state_taps, heads, chans)
        return small, lora, zx, y, gained, squares, states

    def cotangents(row, cot, gained):
        low = (dot(cot, out_up, NT) * row_data[row][1]).astype(BF16)
        grad = dot(cot, out_weight, NT) + dot(low, out_down, NT)
        return low, grad, jnp.sum(grad * gained.astype(F32), axis=1)

    def project_out(row, gained):
        low = (dot(gained, out_down) * row_data[row][1]).astype(BF16)
        return (dot(gained, out_weight) + dot(low, out_up)).astype(BF16)

    def out_gradients(row, low, gained, scale):
        select = row_data[row][1]
        scaled_low = (low.astype(F32) * scale[:, None]).astype(BF16)
        lora_back = (dot(gained, out_down) * select * scale[:, None]).astype(BF16)
        return (
            lax.dot_general(gained, scaled_low, TN, preferred_element_type=F32),
            lax.dot_general(lora_back, cots[row], TN, preferred_element_type=F32),
        )

    def backward(row, gm):
        ends, select = row_data[row]
        small, lora, zx, y, gained, _, states = fw[row]
        return mixer_backward(
            ends, zx, small, gm, y, states, rks[row], conv_taps, state_taps, heads, chans
        )

    def in_gradients(row, dzx, mid):
        return (
            lax.dot_general(dzx, fw[row][1], TN, preferred_element_type=F32),
            lax.dot_general(normed[row], mid, TN, preferred_element_type=F32),
        )

    def project_in(row, dzx, dsmall):
        return (dot(dzx, zx_weight, NT) + dot(dsmall, small_weight, NT)).astype(BF16)

    fw = [forward(0, normed[0]), None]
    came_cot = links.send_other(after(cotangent, fw[0][4]))
    back = [cotangents(0, after(cots[0], fw[0][4]), fw[0][4]), None]
    fw[1] = forward(1, after(normed[1], back[0][1]))
    cots[1] = links.gather_other(after(came_cot, fw[1][4]))
    back[1] = cotangents(1, cots[1], fw[1][4])
    stats = [jnp.stack([fw[r][5][0], back[r][2]]) for r in range(2)]
    stats = links.sum_stats(stats[0], stats[1])
    sent_out, came_out = links.reduce_other(project_out(1, after(fw[1][4], back[1][2])))
    inv, rks = [], []
    for r in range(2):
        scale = lax.rsqrt(stats[r][0] / inner + EPS)
        kappa = scale * scale * (stats[r][1] / inner)
        inv.append(scale)
        rks.append(
            jnp.concatenate(
                [jnp.broadcast_to(scale[:, None], (ROW_LEN, 128)), jnp.broadcast_to(kappa[:, None], (ROW_LEN, 128))],
                axis=1,
            )
        )
    grads_1 = out_gradients(1, back[1][0], fw[1][4], inv[1])
    grads_0 = out_gradients(0, back[0][0], fw[0][4], inv[0])
    down_total, up_total = [a + b for a, b in zip(grads_0, grads_1)]
    out_chain = FactorSum(up_total.T, down_total)

    gm_1 = after(out_chain.cover(back[1][1]), sent_out, down_total)
    dzx_1, dbc_1, ddt_1 = backward(1, gm_1)
    dzx_1 = out_chain.cover(after(dzx_1, came_out))
    mid_1 = (dot(dzx_1, in_up, NT) * row_data[1][1]).astype(BF16)
    sent_in, came_in = links.reduce_other(project_in(1, dzx_1, jnp.concatenate([dbc_1, ddt_1, mid_1], axis=1)))
    in_1 = in_gradients(1, out_chain.cover(after(dzx_1, sent_in)), mid_1)
    gm_0 = out_chain.cover(after(back[0][1], sent_in, *in_1))
    dzx_0, dbc_0, ddt_0 = backward(0, gm_0)
    dzx_0 = out_chain.cover(after(dzx_0, came_in))
    mid_0 = (dot(dzx_0, in_up, NT) * row_data[0][1]).astype(BF16)
    in_0 = in_gradients(0, dzx_0, out_chain.cover(mid_0))
    in_up_total, in_down_total = [a + b for a, b in zip(in_1, in_0)]
    in_chain = FactorSum(in_down_total, in_up_total)

    dzx_0 = after(in_chain.cover(dzx_0), in_up_total)
    whole_in = project_in(0, dzx_0, jnp.concatenate([dbc_0, ddt_0, mid_0], axis=1))
    gained_0 = after(in_chain.cover(fw[0][4]), whole_in)
    whole_out = project_out(0, gained_0)
    out_sum = links.reduce_own(in_chain.cover(whole_out), came_out)
    output = (residual + links.mine(inv[0])[:, None] * out_sum).astype(BF16)
    grad_normed = links.reduce_own(in_chain.cover(after(whole_in, output)), came_in)
    scaled = grad_normed * norm_gain
    grad_tokens = (
        cotangent.astype(F32)
        + inv_rms * scaled
        - residual * inv_rms**3 * (jnp.sum(scaled * residual, axis=1, keepdims=True) / model)
    )
    out_up_sum, out_down_sum = out_chain.finish()
    in_down_sum, in_up_sum = in_chain.finish()
    out_up_sum, in_up_sum = out_up_sum.T, in_up_sum.T
    return (
        output,
        grad_tokens,
        in_down_sum.reshape(model, adapters, rank),
        in_up_sum.reshape(adapters, rank, 2, width),
        out_down_sum.reshape(width, adapters, rank),
        out_up_sum.reshape(adapters, rank, model),
    )


def solution(mesh):
    return jax.shard_map(
        on_device,
        mesh=mesh,
        in_specs=(
            P(("dp", "tensor"), None), P(("dp", "tensor"), None), P(), P(), P(), P(),
            P(None, None, "tensor"), P(), P(None, "tensor"), P(None, "tensor"), P(), P(None, "tensor"),
            P("tensor"), P("tensor", None), P(), P(None, None, None, "tensor"), P("tensor", None, None), P(),
        ),
        out_specs=(
            P(("dp", "tensor"), None), P(("dp", "tensor"), None), P(),
            P(None, None, None, "tensor"), P("tensor", None, None), P(),
        ),
        check_vma=False,
    )
```

```python
import functools

import jax
import jax.numpy as jnp
from jax import lax
from jax.experimental import pallas as pl
from jax.experimental.pallas import tpu as pltpu
from jax.sharding import PartitionSpec as P


F32, BF16 = jnp.float32, jnp.bfloat16
L = 128
HEAD = 64
HALO = 8
NN = (((1,), (0,)), ((), ()))
NT = (((1,), (1,)), ((), ()))
TN = (((0,), (0,)), ((), ()))


def mm(a, b, dims=NN):
    return lax.dot_general(a, b, dims, preferred_element_type=F32)


def split2(v):
    hi = v.astype(BF16)
    return hi, (v - hi.astype(F32)).astype(BF16)


def split3(v):
    hi = v.astype(BF16)
    rest = v - hi.astype(F32)
    mid = rest.astype(BF16)
    return hi, mid, (rest - mid.astype(F32)).astype(BF16)


def sigmoid(v):
    return 0.5 * jnp.tanh(0.5 * v) + 0.5


def starts_of(pos, ends, count):
    start = jnp.zeros_like(pos)
    for k in range(count - 1):
        start = jnp.where(pos >= ends[k], jnp.maximum(start, ends[k]), start)
    return start


def scalar_start(pos, ends, count):
    start = jnp.int32(0)
    for k in range(count - 1):
        start = jnp.where(pos >= ends[k], jnp.maximum(start, ends[k]), start)
    return start


def chunk_geometry(t0, ends, count):
    rows = t0 + lax.broadcasted_iota(jnp.int32, (L, L), 0)
    cols = t0 + lax.broadcasted_iota(jnp.int32, (L, L), 1)
    row_start = starts_of(rows, ends, count)
    col_start = starts_of(cols, ends, count)
    last_start = scalar_start(t0 + (L - 1), ends, count)
    return rows, cols, row_start, col_start, last_start


def conv_tile(ext, taps, within):
    total = ext[HALO:] * taps[3:4] + taps[4:5]
    for lag in range(1, 4):
        moved = pltpu.roll(ext, lag, 0)[HALO:]
        total = total + jnp.where(within >= lag, moved, 0.0) * taps[3 - lag : 4 - lag]
    return total


def conv_back(ext, taps, ok):
    size = ext.shape[0]
    total = ext[:L] * taps[3:4]
    for lag in range(1, 4):
        moved = pltpu.roll(ext, size - lag, 0)[:L]
        total = total + jnp.where(ok[lag - 1], moved, 0.0) * taps[3 - lag : 4 - lag]
    return total


def step_terms(dt_raw, bias, rate, low_mask):
    raw = dt_raw + bias
    dt = jnp.maximum(raw, 0.0) + jnp.log1p(jnp.exp(-jnp.abs(raw)))
    decay = dt * rate
    cum = sum(mm(low_mask, part) for part in split3(decay))
    return raw, dt, cum


def lane_pair(low, value, h):
    first = jnp.broadcast_to(value[:, h : h + 1], (L, 128))
    second = jnp.broadcast_to(value[:, h + 1 : h + 2], (L, 128))
    return first, second, jnp.where(low, first, second)


def forward_kernel(
    count, ends, z_ref, x_ref, bc_ref, dt_ref, sel_ref, down_ref,
    taps_ref, bct_ref, head_ref, chan_ref,
    y_ref, g_ref, sum_ref, st_ref, state, xprev, bcprev,
):
    c = pl.program_id(0)
    width = x_ref.shape[1]
    pairs = width // 128

    @pl.when(c == 0)
    def _():
        state[...] = jnp.zeros_like(state)
        xprev[...] = jnp.zeros_like(xprev)
        bcprev[...] = jnp.zeros_like(bcprev)

    t0 = c * L
    rows, cols, row_start, col_start, last_start = chunk_geometry(t0, ends, count)
    within = rows - row_start
    mask = (row_start == col_start) & (cols <= rows)
    low_mask = jnp.where(mask, 1.0, 0.0).astype(BF16)
    contin = row_start < t0
    tail = row_start == last_start
    keep = jnp.where(last_start < t0, 1.0, 0.0).astype(F32)
    low = lax.broadcasted_iota(jnp.int32, (L, 128), 1) < HEAD

    bc_halves = []
    for half in range(2):
        cut = slice(half * 128, half * 128 + 128)
        ext = jnp.concatenate([bcprev[:, cut], bc_ref[:, cut]], axis=0)
        pre = conv_tile(ext, bct_ref[:, cut], within)
        bc_halves.append((pre * sigmoid(pre)))
    b_mat, c_mat = bc_halves
    b_low, c_low = b_mat.astype(BF16), c_mat.astype(BF16)
    b_turn = b_mat.T.astype(BF16)
    scores = jnp.where(mask, mm(c_low, b_low, NT), 0.0)

    _, dt, cum = step_terms(dt_ref[...], head_ref[0:1], head_ref[1:2], low_mask)
    cum_turn = cum.T

    squares = jnp.zeros((L, 128), F32)
    for p in range(pairs):
        cut = slice(p * 128, p * 128 + 128)
        ext = jnp.concatenate([xprev[:, cut], x_ref[:, cut]], axis=0)
        pre = conv_tile(ext, taps_ref[:, cut], within)
        xc = pre * sigmoid(pre)
        c0, c1, c_both = lane_pair(low, cum, 2 * p)
        _, _, dt_both = lane_pair(low, dt, 2 * p)
        xt = xc * dt_both
        xb = xt.astype(BF16)
        zero = jnp.zeros_like(xb)
        x2 = jnp.concatenate([jnp.where(low, xb, zero), jnp.where(low, zero, xb)], axis=0)
        g0 = (scores * jnp.exp(jnp.minimum(c0 - cum_turn[2 * p : 2 * p + 1], 0.0))).astype(BF16)
        g1 = (scores * jnp.exp(jnp.minimum(c1 - cum_turn[2 * p + 1 : 2 * p + 2], 0.0))).astype(BF16)
        inside = mm(jnp.concatenate([g0, g1], axis=1), x2)
        old = state[:, cut]
        old_low = old.astype(BF16)
        st_ref[0, :, cut] = old_low
        carried = jnp.where(contin, jnp.exp(c_both), 0.0)
        y = inside + mm(c_low, old_low) * carried
        y_ref[:, cut] = y
        c_last = c_both[L - 1 :, :]
        tail_w = jnp.where(tail, jnp.exp(c_last - c_both), 0.0)
        state[:, cut] = (keep * jnp.exp(c_last)) * old + mm(b_turn, (xt * tail_w).astype(BF16))
        z = z_ref[:, cut]
        gated = (y + chan_ref[0:1, cut] * xc) * (z * sigmoid(z))
        gained = gated * chan_ref[1:2, cut]
        g_ref[:, cut] = gained.astype(BF16)
        squares = squares + gated * gated
    ones = jnp.ones((8, 128), BF16)
    sq_row = sum(mm(ones, part, NT) for part in split3(squares))
    sum_ref[...] = sq_row
    g_ref[:, width:] = (mm(g_ref[:, :width], down_ref[...]) * sel_ref[...]).astype(BF16)
    xprev[...] = x_ref[L - HALO :, :]
    bcprev[...] = bc_ref[L - HALO :, :]


def backward_kernel(
    count, seq, ends, z_ref, x_ref, xh_ref, bc_ref, bch_ref, dt_ref, gm_ref, y_ref, st_ref, rk_ref,
    lora_ref, nb_ref, sel_ref, up_ref, taps_ref, bct_ref, head_ref, chan_ref,
    dzx_ref, inup_ref, indown_ref, dstate, dnext, dbnext, ends_row,
):
    g = pl.program_id(0)
    c = pl.num_programs(0) - 1 - g
    width = x_ref.shape[1]
    pairs = width // 128

    @pl.when(g == 0)
    def _():
        dstate[...] = jnp.zeros_like(dstate)
        dnext[...] = jnp.zeros_like(dnext)
        dbnext[...] = jnp.zeros_like(dbnext)
        ends_row[...] = jnp.zeros_like(ends_row)
        inup_ref[...] = jnp.zeros_like(inup_ref)
        indown_ref[...] = jnp.zeros_like(indown_ref)

    t0 = c * L
    rows, cols, row_start, col_start, last_start = chunk_geometry(t0, ends, count)
    within = rows - row_start
    same = row_start == col_start
    low_mask = jnp.where(same & (cols <= rows), 1.0, 0.0).astype(BF16)
    up = same & (rows <= cols)
    up_mask = jnp.where(up, 1.0, 0.0).astype(BF16)
    contin = row_start < t0
    tail = row_start == last_start
    keep = jnp.where(last_start < t0, 1.0, 0.0).astype(F32)
    lane = lax.broadcasted_iota(jnp.int32, (L, 128), 1)
    sub = lax.broadcasted_iota(jnp.int32, (L, 128), 0)
    low = lane < HEAD
    ok = [
        (rows + lag < seq) & (starts_of(rows + lag, ends, count) <= rows) for lag in range(1, 4)
    ]

    parts = []
    for half in range(2):
        cut = slice(half * 128, half * 128 + 128)
        ext = jnp.concatenate([bch_ref[:, cut], bc_ref[:, cut]], axis=0)
        pre = conv_tile(ext, bct_ref[:, cut], within)
        sg = sigmoid(pre)
        act = pre * sg
        parts.append((act, sg + act * (1.0 - sg)))
    (b_mat, b_slope), (c_mat, c_slope) = parts
    b_low, c_low = b_mat.astype(BF16), c_mat.astype(BF16)
    c_turn = c_mat.T.astype(BF16)
    scores = jnp.where(up, mm(b_low, c_low, NT), 0.0)

    raw, dt, cum = step_terms(dt_ref[...], head_ref[0:1], head_ref[1:2], low_mask)
    cum_turn = cum.T
    inv, kappa = rk_ref[:, :128], rk_ref[:, 128:]

    d_scores = jnp.zeros((L, L), F32)
    d_b = jnp.zeros((L, 128), F32)
    d_c = jnp.zeros((L, 128), F32)
    d_cum = jnp.zeros((L, 128), F32)
    d_dt = jnp.zeros((L, 128), F32)
    d_end = jnp.zeros((8, 128), F32)
    for p in range(pairs):
        cut = slice(p * 128, p * 128 + 128)
        pick = jnp.where(lane == 2 * p + jnp.where(sub >= HEAD, 1, 0), 1.0, 0.0).astype(BF16)
        ext = jnp.concatenate([xh_ref[:, cut], x_ref[:, cut]], axis=0)
        taps = taps_ref[:, cut]
        pre = conv_tile(ext, taps, within)
        sg = sigmoid(pre)
        xc = pre * sg
        skip = chan_ref[0:1, cut]
        z = z_ref[:, cut]
        sz = sigmoid(z)
        sil = z * sz
        y = y_ref[:, cut]
        yt = y + skip * xc
        gg = inv * (gm_ref[:, cut] * chan_ref[1:2, cut] - kappa * (yt * sil))
        dzx_ref[:, cut] = (gg * yt * (sz + sil * (1.0 - sz))).astype(BF16)
        dyt = gg * sil
        dyb = dyt.astype(BF16)
        zero = jnp.zeros_like(dyb)
        dy2 = jnp.concatenate([jnp.where(low, dyb, zero), jnp.where(low, zero, dyb)], axis=0)
        c0, c1, c_both = lane_pair(low, cum, 2 * p)
        _, _, dt_both = lane_pair(low, dt, 2 * p)
        xt = xc * dt_both
        xb = xt.astype(BF16)
        dg = mm(xb, dy2, NT)
        w0 = jnp.exp(jnp.minimum(cum_turn[2 * p : 2 * p + 1] - c0, 0.0))
        w1 = jnp.exp(jnp.minimum(cum_turn[2 * p + 1 : 2 * p + 2] - c1, 0.0))
        d_scores = d_scores + dg[:, :L] * w0 + dg[:, L:] * w1
        gt = jnp.concatenate([(scores * w0).astype(BF16), (scores * w1).astype(BF16)], axis=1)
        carried = jnp.where(contin, jnp.exp(c_both), 0.0)
        c_last = c_both[L - 1 :, :]
        tail_w = jnp.where(tail, jnp.exp(c_last - c_both), 0.0)
        ds = dstate[:, cut]
        ds_low = ds.astype(BF16)
        dxt = mm(gt, dy2) + mm(b_low, ds_low) * tail_w
        dyc = (dyt * carried).astype(BF16)
        st = st_ref[0, :, cut]
        d_c = d_c + mm(dyc, st, NT)
        d_b = d_b + mm((xt * tail_w).astype(BF16), ds_low, NT)
        ds_new = (keep * jnp.exp(c_last)) * ds + mm(c_turn, dyc)
        dstate[:, cut] = ds_new
        both = jnp.sum(ds_new * st.astype(F32), axis=0, keepdims=True)
        both = jnp.broadcast_to(both, (8, 128))
        d_end = d_end + sum(mm(part, pick) for part in split2(both))
        v = dyb.astype(F32) * y - xb.astype(F32) * dxt
        d_cum = d_cum + sum(mm(part, pick) for part in split2(v))
        d_dt = d_dt + sum(mm(part, pick) for part in split2(dxt * xc))
        dpre = (skip * dyt + dt_both * dxt) * (sg + xc * (1.0 - sg))
        ext = jnp.concatenate([dpre, dnext[:, cut]], axis=0)
        dzx_ref[:, slice(width + p * 128, width + p * 128 + 128)] = conv_back(ext, taps, ok).astype(BF16)
        dnext[:, cut] = dpre[:HALO]

    d_scores = jnp.where(up, d_scores, 0.0)
    d_b = d_b + mm(d_scores.astype(BF16), c_low)
    d_c = d_c + mm(d_scores.T.astype(BF16), b_low)
    for half, (grad, slope) in enumerate(((d_b, b_slope), (d_c, c_slope))):
        cut = slice(half * 128, half * 128 + 128)
        dpre = grad * slope
        ext = jnp.concatenate([dpre, dbnext[:, cut]], axis=0)
        place = slice(2 * width + half * 128, 2 * width + half * 128 + 128)
        dzx_ref[:, place] = conv_back(ext, bct_ref[:, cut], ok).astype(BF16)
        dbnext[:, cut] = dpre[:HALO]
    d_cum = d_cum + jnp.where(sub == L - 1, ends_row[0:1, :], 0.0)
    ends_row[...] = d_end
    d_decay = sum(mm(up_mask, part) for part in split3(d_cum))
    d_raw = (d_dt + head_ref[1:2] * d_decay) * sigmoid(raw)
    dzx_ref[:, 2 * width + 256 : 2 * width + 384] = d_raw.astype(BF16)
    mid = mm(dzx_ref[:, : 2 * width], up_ref[...], NT) * sel_ref[...]
    dzx_ref[:, 2 * width + 384 :] = mid.astype(BF16)
    mid_turn = mid.T.astype(BF16)
    lora_turn = lora_ref[...].astype(F32).T.astype(BF16)
    for k in range(0, 2 * width, 256):
        cut = slice(k, k + 256)
        inup_ref[:, cut] += mm(lora_turn, dzx_ref[:, cut])
    for k in range(0, nb_ref.shape[1], 256):
        cut = slice(k, k + 256)
        indown_ref[:, cut] += mm(mid_turn, nb_ref[:, cut])


def mixer_forward(ends, zx, small, select, out_down, taps, bctaps, heads, chans):
    seq, width = zx.shape[0], chans.shape[1]
    count = ends.shape[0] - 1
    chunks = seq // L
    place = lambda c, e: lax.rem(c + e[count] * (chunks // 2), chunks)
    fixed = lambda shape: pl.BlockSpec(shape, lambda c, e: (0,) * len(shape))
    blk = lambda w, first=0: pl.BlockSpec((L, w), lambda c, e: (place(c, e), first // w))
    return pl.pallas_call(
        functools.partial(forward_kernel, count),
        grid_spec=pltpu.PrefetchScalarGridSpec(
            num_scalar_prefetch=1,
            grid=(chunks,),
            in_specs=[
                blk(width), blk(width, width), blk(256), blk(128, 256), blk(128), fixed((width, 128)),
                fixed((5, width)), fixed((5, 256)), fixed((2, 128)), fixed((2, width)),
            ],
            out_specs=[
                blk(width), blk(width + 128), pl.BlockSpec((8, L), lambda c, e: (0, place(c, e))),
                pl.BlockSpec((1, 128, width), lambda c, e: (c, 0, 0)),
            ],
            scratch_shapes=[
                pltpu.VMEM((128, width), F32), pltpu.VMEM((HALO, width), F32), pltpu.VMEM((HALO, 256), F32),
            ],
        ),
        out_shape=[
            jax.ShapeDtypeStruct((seq, width), F32),
            jax.ShapeDtypeStruct((seq, width + 128), BF16),
            jax.ShapeDtypeStruct((8, seq), F32),
            jax.ShapeDtypeStruct((chunks, 128, width), BF16),
        ],
        compiler_params=pltpu.CompilerParams(dimension_semantics=("arbitrary",)),
        cost_estimate=pl.CostEstimate(
            flops=seq * width * 1200, bytes_accessed=seq * width * 16, transcendentals=seq * width * 6
        ),
        name="mixer_forward",
    )(ends, zx, zx, small, small, select, out_down, taps, bctaps, heads, chans)


def mixer_backward(ends, zx, small, gm, y, states, rk, lora, normed, select, in_up, taps, bctaps, heads, chans):
    seq, width = gm.shape
    model = normed.shape[1]
    count = ends.shape[0] - 1
    chunks = seq // L
    last = chunks - 1
    step = L // HALO
    place = lambda c, e: lax.rem(c + e[count] * (chunks // 2), chunks)
    fixed = lambda shape: pl.BlockSpec(shape, lambda g, e: (0,) * len(shape))
    blk = lambda w, first=0: pl.BlockSpec((L, w), lambda g, e: (place(last - g, e), first // w))
    halo = lambda w, first=0: pl.BlockSpec(
        (HALO, w), lambda g, e: (place(jnp.maximum(last - g - 1, 0), e) * step + step - 1, first // w)
    )
    return pl.pallas_call(
        functools.partial(backward_kernel, count, seq),
        grid_spec=pltpu.PrefetchScalarGridSpec(
            num_scalar_prefetch=1,
            grid=(chunks,),
            in_specs=[
                blk(width), blk(width, width), halo(width, width), blk(256), halo(256), blk(128, 256), blk(width), blk(width),
                pl.BlockSpec((1, 128, width), lambda g, e: (last - g, 0, 0)), blk(256),
                blk(128), blk(model), blk(128), fixed((128, 2 * width)),
                fixed((5, width)), fixed((5, 256)), fixed((2, 128)), fixed((2, width)),
            ],
            out_specs=[blk(2 * width + 512), fixed((128, 2 * width)), fixed((128, model))],
            scratch_shapes=[
                pltpu.VMEM((128, width), F32), pltpu.VMEM((HALO, width), F32), pltpu.VMEM((HALO, 256), F32),
                pltpu.VMEM((8, 128), F32),
            ],
        ),
        out_shape=[
            jax.ShapeDtypeStruct((seq, 2 * width + 512), BF16),
            jax.ShapeDtypeStruct((128, 2 * width), F32),
            jax.ShapeDtypeStruct((128, model), F32),
        ],
        compiler_params=pltpu.CompilerParams(dimension_semantics=("arbitrary",)),
        cost_estimate=pl.CostEstimate(
            flops=seq * width * 3000, bytes_accessed=seq * width * 24, transcendentals=seq * width * 8
        ),
        name="mixer_backward",
    )(
        ends, zx, zx, zx, small, small, small, gm, y, states, rk, lora, normed, select, in_up,
        taps, bctaps, heads, chans,
    )


EPS = 1e-05
ROW_LEN = 1024


def dot(a, b, dims=NN):
    return lax.dot_general(a, b, dims, preferred_element_type=F32)


def row_places(core, flipped):
    shift = core * (ROW_LEN // 2) if flipped else 0
    return jnp.remainder(jnp.arange(ROW_LEN, dtype=jnp.int32) + shift, ROW_LEN)


def row_select(ends, ids, places, columns):
    segment = jnp.sum((places[:, None] >= ends[None, :]).astype(jnp.int32), axis=1)
    member = segment[:, None] == jnp.arange(ends.shape[0], dtype=jnp.int32)[None, :]
    adapter = jnp.sum(jnp.where(member, ids[None, :], 0), axis=1)
    return (adapter[:, None] == columns[None, :]).astype(F32)


def flip(v):
    half = v.shape[-1] // 2
    return jnp.concatenate([v[..., half:], v[..., :half]], axis=-1)


class PairedLinks:
    flipped = True

    def __init__(self):
        me = lax.axis_index("tensor")
        self.own_row, self.core = me // 2, me % 2
        self.across = [(i, i ^ 2) for i in range(4)]
        self.beside = [(i, i ^ 1) for i in range(4)]

    def far(self, v):
        return lax.ppermute(v, "tensor", self.across)

    def near(self, v):
        return lax.ppermute(v, "tensor", self.beside)

    def gather_own(self, v):
        return jnp.concatenate([v, self.near(v)], axis=0)

    def send_other(self, v):
        return self.far(v)

    def gather_other(self, came):
        return jnp.concatenate([came, self.near(came)], axis=0)

    def sum_stats(self, own, other):
        both = jnp.stack([own, other])
        both = both + flip(self.near(both))
        came = self.far(both)
        return both[0] + came[1], both[1] + came[0]

    def reduce_near(self, whole):
        half = ROW_LEN // 2
        second = self.near(whole[half:])
        return whole[:half].astype(F32) + second.astype(F32)

    def reduce_other(self, whole):
        sent = self.reduce_near(whole).astype(BF16)
        return sent, self.far(sent)

    def reduce_own(self, whole, came):
        return self.reduce_near(whole) + came.astype(F32)

    def mine(self, own_stat):
        return own_stat[: ROW_LEN // 2]


class GroupLinks:
    flipped = False

    def __init__(self, parts, rows):
        me = lax.axis_index("tensor")
        per_row = parts // rows
        self.own_row, self.core = me // per_row, me % per_row
        self.per_row = per_row

    def gather_row(self, v, row):
        whole = lax.all_gather(v, "tensor", axis=0, tiled=True).reshape(2, ROW_LEN, v.shape[1])
        return lax.dynamic_index_in_dim(whole, row, 0, False)

    def gather_own(self, v):
        return self.gather_row(v, self.own_row)

    def send_other(self, v):
        return v

    def gather_other(self, v):
        return self.gather_row(v, 1 - self.own_row)

    def sum_stats(self, own, other):
        first = jnp.where(self.own_row == 0, own, other)
        second = jnp.where(self.own_row == 0, other, own)
        total = lax.psum(jnp.stack([first, second]), "tensor")
        return (
            lax.dynamic_index_in_dim(total, self.own_row, 0, False),
            lax.dynamic_index_in_dim(total, 1 - self.own_row, 0, False),
        )

    def reduce_other(self, whole):
        return whole, whole

    def reduce_own(self, own, other):
        first = jnp.where(self.own_row == 0, own, other)
        second = jnp.where(self.own_row == 0, other, own)
        whole = jnp.concatenate([first, second], axis=0)
        return lax.psum_scatter(whole, "tensor", scatter_dimension=0, tiled=True).astype(F32)

    def mine(self, own_stat):
        size = ROW_LEN // self.per_row
        return lax.dynamic_slice_in_dim(own_stat, self.core * size, size, 0)


def after(v, *done):
    return lax.optimization_barrier((v,) + done)[0]


def exchange_steps(axis, wide):
    size = lax.axis_size(axis)
    assert size & (size - 1) == 0
    steps, base = [], 1
    while base < size:
        ways = 4 if wide and base > 1 and size >= 4 * base else 2
        digit = (lax.axis_index(axis) // base) % ways
        pairs = [[(i, i ^ (a * base)) for i in range(size)] for a in range(1, ways)]
        steps.append((axis, digit, pairs))
        base *= ways
    return steps


def piece_of(v, which, ways):
    size = v.shape[0] // ways
    return lax.dynamic_slice_in_dim(v, which * size, size, 0)


def scatter_sum(arrays, step):
    axis, digit, pairs = step
    ways = len(pairs) + 1
    came = []
    for a in range(1, ways):
        sent = jnp.concatenate([piece_of(v, digit ^ a, ways) for v in arrays], axis=0)
        came.append(lax.ppermute(sent.astype(BF16), axis, pairs[a - 1]))
    sums, first = [], 0
    for v in arrays:
        size = v.shape[0] // ways
        total = piece_of(v, digit, ways)
        for block in came:
            total = total + block[first : first + size].astype(F32)
        sums.append(total)
        first += size
    return sums


def gather_pieces(arrays, step):
    axis, digit, pairs = step
    ways = len(pairs) + 1
    sent = jnp.concatenate(arrays, axis=0)
    blocks = [sent] + [lax.ppermute(sent, axis, pairs[a - 1]) for a in range(1, ways)]
    wholes, first = [], 0
    for v in arrays:
        parts = [block[first : first + v.shape[0]] for block in blocks]
        first += v.shape[0]
        placed = []
        for q in range(ways):
            value = parts[q]
            for d in range(1, ways):
                value = jnp.where(digit == d, parts[q ^ d], value)
            placed.append(value)
        wholes.append(jnp.concatenate(placed, axis=0))
    return wholes


class FactorSum:
    def __init__(self, shared, split):
        self.near, self.far = exchange_steps("tensor", False), exchange_steps("dp", True)
        self.arrays, self.split, self.done = [shared], split, 0

    def hop(self):
        near, far = len(self.near), len(self.far)
        at, total = self.done, 2 * (near + far)
        if at == total:
            return
        if at == near:
            self.arrays = self.arrays + [self.split]
        if at == near + far:
            self.arrays = [v.astype(BF16) for v in self.arrays]
        steps = self.near + self.far
        if at < near + far:
            self.arrays = scatter_sum(self.arrays, steps[at])
        else:
            self.arrays = gather_pieces(self.arrays, steps[total - 1 - at])
        self.done += 1
        if self.done == near + 2 * far:
            self.split = self.arrays[1]
            self.arrays = self.arrays[:1]

    def cover(self, v):
        v, *self.arrays = lax.optimization_barrier((v, *self.arrays))
        self.hop()
        return v

    def finish(self):
        while self.done < 2 * (len(self.near) + len(self.far)):
            self.hop()
        return self.arrays[0].astype(F32), self.split.astype(F32)


def on_device(
    tokens, cotangent, lengths, ids, deal, norm_gain, zx_weight, state_weight, step_weight,
    conv_taps, state_taps, head_values, gated_gain, out_weight, in_down, in_up, out_down, out_up,
):
    tok_dev, model = tokens.shape
    parts = lax.axis_size("tensor")
    rows = tok_dev * parts // ROW_LEN
    assert rows == 2
    links = PairedLinks() if parts == 4 else GroupLinks(parts, rows)
    adapters, rank = in_down.shape[1:]
    reduced = adapters * rank
    width = zx_weight.shape[2]
    inner = width * parts
    heads_here = width // HEAD
    in_down = in_down.reshape(model, reduced)
    in_up = in_up.reshape(reduced, 2 * width)
    out_down = out_down.reshape(width, reduced)
    out_up = out_up.reshape(reduced, model)
    zx_weight = zx_weight.reshape(model, 2 * width)
    pad = lambda v: jnp.pad(v, ((0, 0), (0, 128 - heads_here)))
    small_weight = jnp.concatenate([state_weight, pad(step_weight), in_down], axis=1)
    proj_weight = jnp.concatenate([zx_weight, small_weight], axis=1)
    back_weight = jnp.concatenate([out_weight, out_up], axis=0)
    heads = jnp.concatenate([pad(head_values[0:1]), pad(-jnp.exp(head_values[1:2]))], axis=0)
    chans = jnp.stack([jnp.repeat(head_values[2], HEAD), gated_gain])
    columns = jnp.arange(reduced, dtype=jnp.int32) // rank

    places = row_places(links.core, links.flipped)
    turn = (links.core if links.flipped else 0) * jnp.ones((1,), jnp.int32)
    base = lax.axis_index("dp") * rows
    row_data = []
    for which in (links.own_row, 1 - links.own_row):
        packed = lax.dynamic_index_in_dim(deal, base + which, 0, False)
        ends = jnp.cumsum(lax.dynamic_index_in_dim(lengths, packed, 0, False))
        row_ids = lax.dynamic_index_in_dim(ids, packed, 0, False)
        select = row_select(ends, row_ids, places, columns)
        row_data.append((jnp.concatenate([ends, turn]).astype(jnp.int32), select))

    residual = tokens.astype(F32)
    inv_rms = lax.rsqrt(jnp.mean(residual * residual, axis=1, keepdims=True) + EPS)
    normed_here = (residual * inv_rms * norm_gain).astype(BF16)
    normed = [links.gather_own(normed_here), links.gather_other(links.send_other(normed_here))]
    cots = [links.gather_own(cotangent), None]

    def forward(row, nb):
        ends, select = row_data[row]
        small = dot(nb, small_weight)
        lora = (small[:, 384:] * select).astype(BF16)
        zx = dot(nb, proj_weight[:, : 2 * width]) + dot(lora, in_up)
        y, gained, squares, states = mixer_forward(
            ends, zx, small, select, out_down, conv_taps, state_taps, heads, chans
        )
        return small, lora, zx, y, gained, squares, states

    def cotangents(row, cot, gained):
        low = (dot(cot, out_up, NT) * row_data[row][1]).astype(BF16)
        grad = dot(cot, out_weight, NT) + dot(low, out_down, NT)
        return low, grad, jnp.sum(grad * gained[:, :width].astype(F32), axis=1)

    def project_out(gained):
        return dot(gained, back_weight).astype(BF16)

    def out_gradients(row, low, gained, scale):
        scaled_low = (low.astype(F32) * scale[:, None]).astype(BF16)
        lora_back = (gained[:, width:].astype(F32) * scale[:, None]).astype(BF16)
        return (
            lax.dot_general(gained[:, :width], scaled_low, TN, preferred_element_type=F32),
            lax.dot_general(cots[row], lora_back, TN, preferred_element_type=F32),
        )

    def backward(row, gm):
        ends, select = row_data[row]
        small, lora, zx, y, _, _, states = fw[row]
        return mixer_backward(
            ends, zx, small, gm, y, states, rks[row], lora, normed[row], select, in_up,
            conv_taps, state_taps, heads, chans,
        )

    def project_in(ext):
        return dot(ext, proj_weight, NT).astype(BF16)

    fw = [forward(0, normed[0]), None]
    came_cot = links.send_other(after(cotangent, fw[0][4]))
    back = [cotangents(0, after(cots[0], fw[0][4]), fw[0][4]), None]
    fw[1] = forward(1, after(normed[1], back[0][1]))
    cots[1] = links.gather_other(after(came_cot, fw[1][4]))
    back[1] = cotangents(1, cots[1], fw[1][4])
    stats = [jnp.stack([fw[r][5][0], back[r][2]]) for r in range(2)]
    stats = links.sum_stats(stats[0], stats[1])
    sent_out, came_out = links.reduce_other(project_out(after(fw[1][4], back[1][2])))
    inv, rks = [], []
    for r in range(2):
        scale = lax.rsqrt(stats[r][0] / inner + EPS)
        kappa = scale * scale * (stats[r][1] / inner)
        inv.append(scale)
        rks.append(
            jnp.concatenate(
                [jnp.broadcast_to(scale[:, None], (ROW_LEN, 128)), jnp.broadcast_to(kappa[:, None], (ROW_LEN, 128))],
                axis=1,
            )
        )
    grads_1 = out_gradients(1, back[1][0], fw[1][4], inv[1])
    grads_0 = out_gradients(0, back[0][0], fw[0][4], inv[0])
    down_total, up_total = [a + b for a, b in zip(grads_0, grads_1)]
    out_up_sum = lax.psum(up_total.astype(BF16), ("dp", "tensor"))
    out_down_sum = lax.psum(down_total.astype(BF16), "dp")

    gm_1 = after(back[1][1], sent_out, down_total, up_total)
    ext_1, *in_1 = backward(1, gm_1)
    sent_in, came_in = links.reduce_other(project_in(after(ext_1, came_out)))
    gm_0 = after(back[0][1], sent_in)
    ext_0, *in_0 = backward(0, gm_0)
    ext_0 = after(ext_0, came_in)
    in_up_total, in_down_total = [(a + b).T for a, b in zip(in_1, in_0)]
    in_chain = FactorSum(in_down_total, in_up_total)

    whole_out = project_out(in_chain.cover(after(fw[0][4], ext_0)))
    whole_in = project_in(in_chain.cover(after(ext_0, whole_out)))
    out_sum = links.reduce_own(whole_out, in_chain.cover(after(came_out, whole_in)))
    output = (residual + links.mine(inv[0])[:, None] * out_sum).astype(BF16)
    grad_normed = links.reduce_own(whole_in, in_chain.cover(after(came_in, output)))
    scaled = grad_normed * norm_gain
    grad_tokens = (
        cotangent.astype(F32)
        + inv_rms * scaled
        - residual * inv_rms**3 * (jnp.sum(scaled * residual, axis=1, keepdims=True) / model)
    )
    grad_tokens = in_chain.cover(grad_tokens)
    in_down_sum, in_up_sum = in_chain.finish()
    out_down_sum = after(out_down_sum, in_down_sum)
    out_up_sum, out_down_sum = out_up_sum.T.astype(F32), out_down_sum.astype(F32)
    in_up_sum = in_up_sum.T
    return (
        output,
        grad_tokens,
        in_down_sum.reshape(model, adapters, rank),
        in_up_sum.reshape(adapters, rank, 2, width),
        out_down_sum.reshape(width, adapters, rank),
        out_up_sum.reshape(adapters, rank, model),
    )


def solution(mesh):
    return jax.shard_map(
        on_device,
        mesh=mesh,
        in_specs=(
            P(("dp", "tensor"), None), P(("dp", "tensor"), None), P(), P(), P(), P(),
            P(None, None, "tensor"), P(), P(None, "tensor"), P(None, "tensor"), P(), P(None, "tensor"),
            P("tensor"), P("tensor", None), P(), P(None, None, None, "tensor"), P("tensor", None, None), P(),
        ),
        out_specs=(
            P(("dp", "tensor"), None), P(("dp", "tensor"), None), P(),
            P(None, None, None, "tensor"), P("tensor", None, None), P(),
        ),
        check_vma=False,
    )
```

```python
import functools

import jax
import jax.numpy as jnp
from jax import lax
from jax.experimental import pallas as pl
from jax.experimental.pallas import tpu as pltpu
from jax.sharding import PartitionSpec as P


F32, BF16 = jnp.float32, jnp.bfloat16
L = 128
HEAD = 64
HALO = 8
NN = (((1,), (0,)), ((), ()))
NT = (((1,), (1,)), ((), ()))
TN = (((0,), (0,)), ((), ()))


def mm(a, b, dims=NN):
    return lax.dot_general(a, b, dims, preferred_element_type=F32)


def split2(v):
    hi = v.astype(BF16)
    return hi, (v - hi.astype(F32)).astype(BF16)


def split3(v):
    hi = v.astype(BF16)
    rest = v - hi.astype(F32)
    mid = rest.astype(BF16)
    return hi, mid, (rest - mid.astype(F32)).astype(BF16)


def sigmoid(v):
    return 0.5 * jnp.tanh(0.5 * v) + 0.5


def starts_of(pos, ends, count):
    start = jnp.zeros_like(pos)
    for k in range(count - 1):
        start = jnp.where(pos >= ends[k], jnp.maximum(start, ends[k]), start)
    return start


def scalar_start(pos, ends, count):
    start = jnp.int32(0)
    for k in range(count - 1):
        start = jnp.where(pos >= ends[k], jnp.maximum(start, ends[k]), start)
    return start


def chunk_geometry(t0, ends, count):
    rows = t0 + lax.broadcasted_iota(jnp.int32, (L, L), 0)
    cols = t0 + lax.broadcasted_iota(jnp.int32, (L, L), 1)
    row_start = starts_of(rows, ends, count)
    col_start = starts_of(cols, ends, count)
    last_start = scalar_start(t0 + (L - 1), ends, count)
    return rows, cols, row_start, col_start, last_start


def conv_tile(ext, taps, within):
    total = ext[HALO:] * taps[3:4] + taps[4:5]
    for lag in range(1, 4):
        moved = pltpu.roll(ext, lag, 0)[HALO:]
        total = total + jnp.where(within >= lag, moved, 0.0) * taps[3 - lag : 4 - lag]
    return total


def conv_back(ext, taps, ok):
    size = ext.shape[0]
    total = ext[:L] * taps[3:4]
    for lag in range(1, 4):
        moved = pltpu.roll(ext, size - lag, 0)[:L]
        total = total + jnp.where(ok[lag - 1], moved, 0.0) * taps[3 - lag : 4 - lag]
    return total


def masked_sum(mask, v):
    hi, mid, low = split3(v)
    twice = jnp.concatenate([mask, mask], axis=1)
    return mm(twice, jnp.concatenate([hi, mid], axis=0)) + mm(mask, low)


def halves(v):
    return jnp.concatenate(split2(v), axis=1)


def step_terms(dt_raw, bias, rate, low_mask):
    raw = dt_raw + bias
    dt = jnp.maximum(raw, 0.0) + jnp.log1p(jnp.exp(-jnp.abs(raw)))
    decay = dt * rate
    return raw, dt, masked_sum(low_mask, decay)


def lane_pair(low, value, h):
    first = jnp.broadcast_to(value[:, h : h + 1], (L, 128))
    second = jnp.broadcast_to(value[:, h + 1 : h + 2], (L, 128))
    return first, second, jnp.where(low, first, second)


def forward_kernel(
    count, ends, z_ref, x_ref, bc_ref, dt_ref, sel_ref, down_ref,
    taps_ref, bct_ref, head_ref, chan_ref,
    y_ref, g_ref, sum_ref, st_ref, state, xprev, bcprev,
):
    c = pl.program_id(0)
    width = x_ref.shape[1]
    pairs = width // 128

    @pl.when(c == 0)
    def _():
        state[...] = jnp.zeros_like(state)
        xprev[...] = jnp.zeros_like(xprev)
        bcprev[...] = jnp.zeros_like(bcprev)

    t0 = c * L
    rows, cols, row_start, col_start, last_start = chunk_geometry(t0, ends, count)
    within = rows - row_start
    mask = (row_start == col_start) & (cols <= rows)
    low_mask = jnp.where(mask, 1.0, 0.0).astype(BF16)
    contin = row_start < t0
    tail = row_start == last_start
    keep = jnp.where(last_start < t0, 1.0, 0.0).astype(F32)
    low = lax.broadcasted_iota(jnp.int32, (L, 128), 1) < HEAD

    bc_halves = []
    for half in range(2):
        cut = slice(half * 128, half * 128 + 128)
        ext = jnp.concatenate([bcprev[:, cut], bc_ref[:, cut]], axis=0)
        pre = conv_tile(ext, bct_ref[:, cut], within)
        bc_halves.append((pre * sigmoid(pre)))
    b_mat, c_mat = bc_halves
    b_low, c_low = b_mat.astype(BF16), c_mat.astype(BF16)
    b_turn = b_mat.T.astype(BF16)
    scores = jnp.where(mask, mm(c_low, b_low, NT), 0.0)

    _, dt, cum = step_terms(dt_ref[...], head_ref[0:1], head_ref[1:2], low_mask)
    cum_turn = cum.T

    squares = jnp.zeros((L, 128), F32)
    for p in range(pairs):
        cut = slice(p * 128, p * 128 + 128)
        ext = jnp.concatenate([xprev[:, cut], x_ref[:, cut]], axis=0)
        pre = conv_tile(ext, taps_ref[:, cut], within)
        xc = pre * sigmoid(pre)
        c0, c1, c_both = lane_pair(low, cum, 2 * p)
        _, _, dt_both = lane_pair(low, dt, 2 * p)
        xt = xc * dt_both
        xb = xt.astype(BF16)
        zero = jnp.zeros_like(xb)
        x2 = jnp.concatenate([jnp.where(low, xb, zero), jnp.where(low, zero, xb)], axis=0)
        g0 = (scores * jnp.exp(jnp.minimum(c0 - cum_turn[2 * p : 2 * p + 1], 0.0))).astype(BF16)
        g1 = (scores * jnp.exp(jnp.minimum(c1 - cum_turn[2 * p + 1 : 2 * p + 2], 0.0))).astype(BF16)
        inside = mm(jnp.concatenate([g0, g1], axis=1), x2)
        old = state[:, cut]
        old_low = old.astype(BF16)
        st_ref[0, :, cut] = old_low
        carried = jnp.where(contin, jnp.exp(c_both), 0.0)
        y = inside + mm(c_low, old_low) * carried
        y_ref[:, cut] = y
        c_last = c_both[L - 1 :, :]
        tail_w = jnp.where(tail, jnp.exp(c_last - c_both), 0.0)
        state[:, cut] = (keep * jnp.exp(c_last)) * old + mm(b_turn, (xt * tail_w).astype(BF16))
        z = z_ref[:, cut]
        gated = (y + chan_ref[0:1, cut] * xc) * (z * sigmoid(z))
        gained = gated * chan_ref[1:2, cut]
        g_ref[:, cut] = gained.astype(BF16)
        squares = squares + gated * gated
    ones = jnp.ones((8, 128), BF16)
    sq_row = sum(mm(ones, part, NT) for part in split3(squares))
    sum_ref[...] = sq_row
    g_ref[:, width:] = (mm(g_ref[:, :width], down_ref[...]) * sel_ref[...]).astype(BF16)
    xprev[...] = x_ref[L - HALO :, :]
    bcprev[...] = bc_ref[L - HALO :, :]


def backward_kernel(
    count, seq, ends, z_ref, x_ref, xh_ref, bc_ref, bch_ref, dt_ref, gm_ref, y_ref, st_ref, rk_ref,
    lora_ref, nb_ref, sel_ref, up_ref, taps_ref, bct_ref, head_ref, chan_ref,
    dzx_ref, inup_ref, indown_ref, dstate, dnext, dbnext, ends_row,
):
    g = pl.program_id(0)
    c = pl.num_programs(0) - 1 - g
    width = x_ref.shape[1]
    pairs = width // 128

    @pl.when(g == 0)
    def _():
        dstate[...] = jnp.zeros_like(dstate)
        dnext[...] = jnp.zeros_like(dnext)
        dbnext[...] = jnp.zeros_like(dbnext)
        ends_row[...] = jnp.zeros_like(ends_row)
        inup_ref[...] = jnp.zeros_like(inup_ref)
        indown_ref[...] = jnp.zeros_like(indown_ref)

    t0 = c * L
    rows, cols, row_start, col_start, last_start = chunk_geometry(t0, ends, count)
    within = rows - row_start
    same = row_start == col_start
    low_mask = jnp.where(same & (cols <= rows), 1.0, 0.0).astype(BF16)
    up = same & (rows <= cols)
    up_mask = jnp.where(up, 1.0, 0.0).astype(BF16)
    contin = row_start < t0
    tail = row_start == last_start
    keep = jnp.where(last_start < t0, 1.0, 0.0).astype(F32)
    lane = lax.broadcasted_iota(jnp.int32, (L, 128), 1)
    sub = lax.broadcasted_iota(jnp.int32, (L, 128), 0)
    low = lane < HEAD
    ok = [
        (rows + lag < seq) & (starts_of(rows + lag, ends, count) <= rows) for lag in range(1, 4)
    ]

    parts = []
    for half in range(2):
        cut = slice(half * 128, half * 128 + 128)
        ext = jnp.concatenate([bch_ref[:, cut], bc_ref[:, cut]], axis=0)
        pre = conv_tile(ext, bct_ref[:, cut], within)
        sg = sigmoid(pre)
        act = pre * sg
        parts.append((act, sg + act * (1.0 - sg)))
    (b_mat, b_slope), (c_mat, c_slope) = parts
    b_low, c_low = b_mat.astype(BF16), c_mat.astype(BF16)
    c_turn = c_mat.T.astype(BF16)
    scores = jnp.where(up, mm(b_low, c_low, NT), 0.0)

    raw, dt, cum = step_terms(dt_ref[...], head_ref[0:1], head_ref[1:2], low_mask)
    cum_turn = cum.T
    inv, kappa = rk_ref[:, :128], rk_ref[:, 128:]

    d_scores = jnp.zeros((L, L), F32)
    d_b = jnp.zeros((L, 128), F32)
    d_c = jnp.zeros((L, 128), F32)
    d_cum = jnp.zeros((L, 128), F32)
    d_dt = jnp.zeros((L, 128), F32)
    d_end = jnp.zeros((8, 128), F32)
    for p in range(pairs):
        cut = slice(p * 128, p * 128 + 128)
        pick = jnp.where(lane == 2 * p + jnp.where(sub >= HEAD, 1, 0), 1.0, 0.0).astype(BF16)
        ext = jnp.concatenate([xh_ref[:, cut], x_ref[:, cut]], axis=0)
        taps = taps_ref[:, cut]
        pre = conv_tile(ext, taps, within)
        sg = sigmoid(pre)
        xc = pre * sg
        skip = chan_ref[0:1, cut]
        z = z_ref[:, cut]
        sz = sigmoid(z)
        sil = z * sz
        y = y_ref[:, cut]
        yt = y + skip * xc
        gg = inv * (gm_ref[:, cut] * chan_ref[1:2, cut] - kappa * (yt * sil))
        dzx_ref[:, cut] = (gg * yt * (sz + sil * (1.0 - sz))).astype(BF16)
        dyt = gg * sil
        dyb = dyt.astype(BF16)
        zero = jnp.zeros_like(dyb)
        dy2 = jnp.concatenate([jnp.where(low, dyb, zero), jnp.where(low, zero, dyb)], axis=0)
        c0, c1, c_both = lane_pair(low, cum, 2 * p)
        _, _, dt_both = lane_pair(low, dt, 2 * p)
        xt = xc * dt_both
        xb = xt.astype(BF16)
        dg = mm(xb, dy2, NT)
        w0 = jnp.exp(jnp.minimum(cum_turn[2 * p : 2 * p + 1] - c0, 0.0))
        w1 = jnp.exp(jnp.minimum(cum_turn[2 * p + 1 : 2 * p + 2] - c1, 0.0))
        d_scores = d_scores + dg[:, :L] * w0 + dg[:, L:] * w1
        gt = jnp.concatenate([(scores * w0).astype(BF16), (scores * w1).astype(BF16)], axis=1)
        carried = jnp.where(contin, jnp.exp(c_both), 0.0)
        c_last = c_both[L - 1 :, :]
        tail_w = jnp.where(tail, jnp.exp(c_last - c_both), 0.0)
        ds = dstate[:, cut]
        ds_low = ds.astype(BF16)
        dxt = mm(gt, dy2) + mm(b_low, ds_low) * tail_w
        dyc = (dyt * carried).astype(BF16)
        st = st_ref[0, :, cut]
        d_c = d_c + mm(dyc, st, NT)
        d_b = d_b + mm((xt * tail_w).astype(BF16), ds_low, NT)
        ds_new = (keep * jnp.exp(c_last)) * ds + mm(c_turn, dyc)
        dstate[:, cut] = ds_new
        both = jnp.sum(ds_new * st.astype(F32), axis=0, keepdims=True)
        both = jnp.broadcast_to(both, (16, 128))
        v = dyb.astype(F32) * y - xb.astype(F32) * dxt
        stacked = jnp.concatenate([halves(v), halves(dxt * xc), halves(both)], axis=0)
        sums = mm(stacked, jnp.concatenate([pick, pick], axis=0))
        d_cum = d_cum + sums[:L]
        d_dt = d_dt + sums[L : 2 * L]
        d_end = d_end + sums[2 * L : 2 * L + 8]
        dpre = (skip * dyt + dt_both * dxt) * (sg + xc * (1.0 - sg))
        ext = jnp.concatenate([dpre, dnext[:, cut]], axis=0)
        dzx_ref[:, slice(width + p * 128, width + p * 128 + 128)] = conv_back(ext, taps, ok).astype(BF16)
        dnext[:, cut] = dpre[:HALO]

    d_scores = jnp.where(up, d_scores, 0.0)
    d_b = d_b + mm(d_scores.astype(BF16), c_low)
    d_c = d_c + mm(d_scores.T.astype(BF16), b_low)
    for half, (grad, slope) in enumerate(((d_b, b_slope), (d_c, c_slope))):
        cut = slice(half * 128, half * 128 + 128)
        dpre = grad * slope
        ext = jnp.concatenate([dpre, dbnext[:, cut]], axis=0)
        place = slice(2 * width + half * 128, 2 * width + half * 128 + 128)
        dzx_ref[:, place] = conv_back(ext, bct_ref[:, cut], ok).astype(BF16)
        dbnext[:, cut] = dpre[:HALO]
    d_cum = d_cum + jnp.where(sub == L - 1, ends_row[0:1, :], 0.0)
    ends_row[...] = d_end
    d_decay = masked_sum(up_mask, d_cum)
    d_raw = (d_dt + head_ref[1:2] * d_decay) * sigmoid(raw)
    dzx_ref[:, 2 * width + 256 : 2 * width + 384] = d_raw.astype(BF16)
    mid = mm(dzx_ref[:, : 2 * width], up_ref[...], NT) * sel_ref[...]
    dzx_ref[:, 2 * width + 384 :] = mid.astype(BF16)
    mid_turn = mid.T.astype(BF16)
    lora_turn = lora_ref[...].astype(F32).T.astype(BF16)
    for k in range(0, 2 * width, 256):
        cut = slice(k, k + 256)
        inup_ref[:, cut] += mm(lora_turn, dzx_ref[:, cut])
    for k in range(0, nb_ref.shape[1], 256):
        cut = slice(k, k + 256)
        indown_ref[:, cut] += mm(mid_turn, nb_ref[:, cut])


def mixer_forward(ends, zx, small, select, out_down, taps, bctaps, heads, chans):
    seq, width = zx.shape[0], chans.shape[1]
    count = ends.shape[0] - 1
    chunks = seq // L
    place = lambda c, e: lax.rem(c + e[count] * (chunks // 2), chunks)
    fixed = lambda shape: pl.BlockSpec(shape, lambda c, e: (0,) * len(shape))
    blk = lambda w, first=0: pl.BlockSpec((L, w), lambda c, e: (place(c, e), first // w))
    return pl.pallas_call(
        functools.partial(forward_kernel, count),
        grid_spec=pltpu.PrefetchScalarGridSpec(
            num_scalar_prefetch=1,
            grid=(chunks,),
            in_specs=[
                blk(width), blk(width, width), blk(256), blk(128, 256), blk(128), fixed((width, 128)),
                fixed((5, width)), fixed((5, 256)), fixed((2, 128)), fixed((2, width)),
            ],
            out_specs=[
                blk(width), blk(width + 128), pl.BlockSpec((8, L), lambda c, e: (0, place(c, e))),
                pl.BlockSpec((1, 128, width), lambda c, e: (c, 0, 0)),
            ],
            scratch_shapes=[
                pltpu.VMEM((128, width), F32), pltpu.VMEM((HALO, width), F32), pltpu.VMEM((HALO, 256), F32),
            ],
        ),
        out_shape=[
            jax.ShapeDtypeStruct((seq, width), F32),
            jax.ShapeDtypeStruct((seq, width + 128), BF16),
            jax.ShapeDtypeStruct((8, seq), F32),
            jax.ShapeDtypeStruct((chunks, 128, width), BF16),
        ],
        compiler_params=pltpu.CompilerParams(dimension_semantics=("arbitrary",)),
        cost_estimate=pl.CostEstimate(
            flops=seq * width * 1200, bytes_accessed=seq * width * 16, transcendentals=seq * width * 6
        ),
        name="mixer_forward",
    )(ends, zx, zx, small, small, select, out_down, taps, bctaps, heads, chans)


def mixer_backward(ends, zx, small, gm, y, states, rk, lora, normed, select, in_up, taps, bctaps, heads, chans):
    seq, width = gm.shape
    model = normed.shape[1]
    count = ends.shape[0] - 1
    chunks = seq // L
    last = chunks - 1
    step = L // HALO
    place = lambda c, e: lax.rem(c + e[count] * (chunks // 2), chunks)
    fixed = lambda shape: pl.BlockSpec(shape, lambda g, e: (0,) * len(shape))
    blk = lambda w, first=0: pl.BlockSpec((L, w), lambda g, e: (place(last - g, e), first // w))
    halo = lambda w, first=0: pl.BlockSpec(
        (HALO, w), lambda g, e: (place(jnp.maximum(last - g - 1, 0), e) * step + step - 1, first // w)
    )
    return pl.pallas_call(
        functools.partial(backward_kernel, count, seq),
        grid_spec=pltpu.PrefetchScalarGridSpec(
            num_scalar_prefetch=1,
            grid=(chunks,),
            in_specs=[
                blk(width), blk(width, width), halo(width, width), blk(256), halo(256), blk(128, 256), blk(width), blk(width),
                pl.BlockSpec((1, 128, width), lambda g, e: (last - g, 0, 0)), blk(256),
                blk(128), blk(model), blk(128), fixed((128, 2 * width)),
                fixed((5, width)), fixed((5, 256)), fixed((2, 128)), fixed((2, width)),
            ],
            out_specs=[blk(2 * width + 512), fixed((128, 2 * width)), fixed((128, model))],
            scratch_shapes=[
                pltpu.VMEM((128, width), F32), pltpu.VMEM((HALO, width), F32), pltpu.VMEM((HALO, 256), F32),
                pltpu.VMEM((8, 128), F32),
            ],
        ),
        out_shape=[
            jax.ShapeDtypeStruct((seq, 2 * width + 512), BF16),
            jax.ShapeDtypeStruct((128, 2 * width), F32),
            jax.ShapeDtypeStruct((128, model), F32),
        ],
        compiler_params=pltpu.CompilerParams(dimension_semantics=("arbitrary",)),
        cost_estimate=pl.CostEstimate(
            flops=seq * width * 3000, bytes_accessed=seq * width * 24, transcendentals=seq * width * 8
        ),
        name="mixer_backward",
    )(
        ends, zx, zx, zx, small, small, small, gm, y, states, rk, lora, normed, select, in_up,
        taps, bctaps, heads, chans,
    )


EPS = 1e-05
ROW_LEN = 1024


def dot(a, b, dims=NN):
    return lax.dot_general(a, b, dims, preferred_element_type=F32)


def row_places(core, flipped):
    shift = core * (ROW_LEN // 2) if flipped else 0
    return jnp.remainder(jnp.arange(ROW_LEN, dtype=jnp.int32) + shift, ROW_LEN)


def row_select(ends, ids, places, columns):
    segment = jnp.sum((places[:, None] >= ends[None, :]).astype(jnp.int32), axis=1)
    member = segment[:, None] == jnp.arange(ends.shape[0], dtype=jnp.int32)[None, :]
    adapter = jnp.sum(jnp.where(member, ids[None, :], 0), axis=1)
    return (adapter[:, None] == columns[None, :]).astype(F32)


def flip(v):
    half = v.shape[-1] // 2
    return jnp.concatenate([v[..., half:], v[..., :half]], axis=-1)


class PairedLinks:
    flipped = True

    def __init__(self):
        me = lax.axis_index("tensor")
        self.own_row, self.core = me // 2, me % 2
        self.across = [(i, i ^ 2) for i in range(4)]
        self.beside = [(i, i ^ 1) for i in range(4)]

    def far(self, v):
        return lax.ppermute(v, "tensor", self.across)

    def near(self, v):
        return lax.ppermute(v, "tensor", self.beside)

    def gather_own(self, v):
        return jnp.concatenate([v, self.near(v)], axis=0)

    def send_other(self, v):
        return self.far(v)

    def gather_other(self, came):
        return jnp.concatenate([came, self.near(came)], axis=0)

    def sum_stats(self, own, other):
        both = jnp.stack([own, other])
        both = both + flip(self.near(both))
        came = self.far(both)
        return both[0] + came[1], both[1] + came[0]

    def reduce_near(self, whole):
        half = ROW_LEN // 2
        second = self.near(whole[half:])
        return whole[:half].astype(F32) + second.astype(F32)

    def reduce_other(self, whole):
        sent = self.reduce_near(whole).astype(BF16)
        return sent, self.far(sent)

    def reduce_own(self, whole, came):
        return self.reduce_near(whole) + came.astype(F32)

    def mine(self, own_stat):
        return own_stat[: ROW_LEN // 2]


class GroupLinks:
    flipped = False

    def __init__(self, parts, rows):
        me = lax.axis_index("tensor")
        per_row = parts // rows
        self.own_row, self.core = me // per_row, me % per_row
        self.per_row = per_row

    def gather_row(self, v, row):
        whole = lax.all_gather(v, "tensor", axis=0, tiled=True).reshape(2, ROW_LEN, v.shape[1])
        return lax.dynamic_index_in_dim(whole, row, 0, False)

    def gather_own(self, v):
        return self.gather_row(v, self.own_row)

    def send_other(self, v):
        return v

    def gather_other(self, v):
        return self.gather_row(v, 1 - self.own_row)

    def sum_stats(self, own, other):
        first = jnp.where(self.own_row == 0, own, other)
        second = jnp.where(self.own_row == 0, other, own)
        total = lax.psum(jnp.stack([first, second]), "tensor")
        return (
            lax.dynamic_index_in_dim(total, self.own_row, 0, False),
            lax.dynamic_index_in_dim(total, 1 - self.own_row, 0, False),
        )

    def reduce_other(self, whole):
        return whole, whole

    def reduce_own(self, own, other):
        first = jnp.where(self.own_row == 0, own, other)
        second = jnp.where(self.own_row == 0, other, own)
        whole = jnp.concatenate([first, second], axis=0)
        return lax.psum_scatter(whole, "tensor", scatter_dimension=0, tiled=True).astype(F32)

    def mine(self, own_stat):
        size = ROW_LEN // self.per_row
        return lax.dynamic_slice_in_dim(own_stat, self.core * size, size, 0)


def after(v, *done):
    return lax.optimization_barrier((v,) + done)[0]


def exchange_steps(axis, wide):
    size = lax.axis_size(axis)
    assert size & (size - 1) == 0
    steps, base = [], 1
    while base < size:
        ways = 4 if wide and base > 1 and size >= 4 * base else 2
        digit = (lax.axis_index(axis) // base) % ways
        pairs = [[(i, i ^ (a * base)) for i in range(size)] for a in range(1, ways)]
        steps.append((axis, digit, pairs))
        base *= ways
    return steps


def piece_of(v, which, ways):
    size = v.shape[0] // ways
    return lax.dynamic_slice_in_dim(v, which * size, size, 0)


def scatter_sum(arrays, step):
    axis, digit, pairs = step
    ways = len(pairs) + 1
    came = []
    for a in range(1, ways):
        sent = jnp.concatenate([piece_of(v, digit ^ a, ways) for v in arrays], axis=0)
        came.append(lax.ppermute(sent.astype(BF16), axis, pairs[a - 1]))
    sums, first = [], 0
    for v in arrays:
        size = v.shape[0] // ways
        total = piece_of(v, digit, ways)
        for block in came:
            total = total + block[first : first + size].astype(F32)
        sums.append(total)
        first += size
    return sums


def gather_pieces(arrays, step):
    axis, digit, pairs = step
    ways = len(pairs) + 1
    sent = jnp.concatenate(arrays, axis=0)
    blocks = [sent] + [lax.ppermute(sent, axis, pairs[a - 1]) for a in range(1, ways)]
    wholes, first = [], 0
    for v in arrays:
        parts = [block[first : first + v.shape[0]] for block in blocks]
        first += v.shape[0]
        placed = []
        for q in range(ways):
            value = parts[q]
            for d in range(1, ways):
                value = jnp.where(digit == d, parts[q ^ d], value)
            placed.append(value)
        wholes.append(jnp.concatenate(placed, axis=0))
    return wholes


class FactorSum:
    def __init__(self, shared, split, summed):
        self.near, self.far = exchange_steps("tensor", False), exchange_steps("dp", True)
        self.arrays, self.split, self.parked, self.done = [shared, summed], split, None, 0

    def hop(self):
        near, far = len(self.near), len(self.far)
        if self.done < 2 * (near + far):
            self.move(near, far)

    def move(self, near, far):
        at, total = self.done, 2 * (near + far)
        if at == near:
            self.parked = self.arrays[1].astype(BF16)
            self.arrays = [self.arrays[0], self.split]
        if at == near + far:
            self.arrays = [v.astype(BF16) for v in self.arrays]
        steps = self.near + self.far
        if at < near + far:
            self.arrays = scatter_sum(self.arrays, steps[at])
        else:
            self.arrays = gather_pieces(self.arrays, steps[total - 1 - at])
        self.done += 1
        if self.done == near + 2 * far:
            self.split = self.arrays[1]
            self.arrays = [self.arrays[0], self.parked]

    def cover(self, v):
        v, *self.arrays = lax.optimization_barrier((v, *self.arrays))
        self.hop()
        return v

    def finish(self):
        while self.done < 2 * (len(self.near) + len(self.far)):
            self.hop()
        return self.arrays[0].astype(F32), self.split.astype(F32), self.arrays[1].astype(F32)


def on_device(
    tokens, cotangent, lengths, ids, deal, norm_gain, zx_weight, state_weight, step_weight,
    conv_taps, state_taps, head_values, gated_gain, out_weight, in_down, in_up, out_down, out_up,
):
    tok_dev, model = tokens.shape
    parts = lax.axis_size("tensor")
    rows = tok_dev * parts // ROW_LEN
    assert rows == 2
    links = PairedLinks() if parts == 4 else GroupLinks(parts, rows)
    adapters, rank = in_down.shape[1:]
    reduced = adapters * rank
    width = zx_weight.shape[2]
    inner = width * parts
    heads_here = width // HEAD
    in_down = in_down.reshape(model, reduced)
    in_up = in_up.reshape(reduced, 2 * width)
    out_down = out_down.reshape(width, reduced)
    out_up = out_up.reshape(reduced, model)
    zx_weight = zx_weight.reshape(model, 2 * width)
    pad = lambda v: jnp.pad(v, ((0, 0), (0, 128 - heads_here)))
    small_weight = jnp.concatenate([state_weight, pad(step_weight), in_down], axis=1)
    proj_weight = jnp.concatenate([zx_weight, small_weight], axis=1)
    back_weight = jnp.concatenate([out_weight, out_up], axis=0)
    heads = jnp.concatenate([pad(head_values[0:1]), pad(-jnp.exp(head_values[1:2]))], axis=0)
    chans = jnp.stack([jnp.repeat(head_values[2], HEAD), gated_gain])
    columns = jnp.arange(reduced, dtype=jnp.int32) // rank

    places = row_places(links.core, links.flipped)
    turn = (links.core if links.flipped else 0) * jnp.ones((1,), jnp.int32)
    base = lax.axis_index("dp") * rows
    row_data = []
    for which in (links.own_row, 1 - links.own_row):
        packed = lax.dynamic_index_in_dim(deal, base + which, 0, False)
        ends = jnp.cumsum(lax.dynamic_index_in_dim(lengths, packed, 0, False))
        row_ids = lax.dynamic_index_in_dim(ids, packed, 0, False)
        select = row_select(ends, row_ids, places, columns)
        row_data.append((jnp.concatenate([ends, turn]).astype(jnp.int32), select))

    residual = tokens.astype(F32)
    inv_rms = lax.rsqrt(jnp.mean(residual * residual, axis=1, keepdims=True) + EPS)
    normed_here = (residual * inv_rms * norm_gain).astype(BF16)
    came_normed = links.send_other(normed_here)
    normed = [lax.optimization_barrier(links.gather_own(normed_here)), None]
    cots = [links.gather_own(cotangent), None]

    def forward(row, nb):
        ends, select = row_data[row]
        small = dot(nb, small_weight)
        lora = (small[:, 384:] * select).astype(BF16)
        zx = dot(nb, proj_weight[:, : 2 * width]) + dot(lora, in_up)
        y, gained, squares, states = mixer_forward(
            ends, zx, small, select, out_down, conv_taps, state_taps, heads, chans
        )
        return small, lora, zx, y, gained, squares, states

    def cotangents(row, cot, gained):
        low = (dot(cot, out_up, NT) * row_data[row][1]).astype(BF16)
        grad = dot(cot, out_weight, NT) + dot(low, out_down, NT)
        return low, grad, jnp.sum(grad * gained[:, :width].astype(F32), axis=1)

    def project_out(gained):
        return dot(gained, back_weight).astype(BF16)

    def out_gradients(row, low, gained, scale):
        scaled_low = (low.astype(F32) * scale[:, None]).astype(BF16)
        lora_back = (gained[:, width:].astype(F32) * scale[:, None]).astype(BF16)
        return (
            lax.dot_general(gained[:, :width], scaled_low, TN, preferred_element_type=F32),
            lax.dot_general(cots[row], lora_back, TN, preferred_element_type=F32),
        )

    def backward(row, gm):
        ends, select = row_data[row]
        small, lora, zx, y, _, _, states = fw[row]
        return mixer_backward(
            ends, zx, small, gm, y, states, rks[row], lora, normed[row], select, in_up,
            conv_taps, state_taps, heads, chans,
        )

    def project_in(ext):
        return dot(ext, proj_weight, NT).astype(BF16)

    fw = [forward(0, normed[0]), None]
    came_cot = links.send_other(after(cotangent, fw[0][4]))
    cots[0] = after(cots[0], fw[0][4])
    back = [cotangents(0, cots[0], fw[0][4]), None]
    normed[1] = after(links.gather_other(after(came_normed, fw[0][4])), back[0][1])
    fw[1] = forward(1, normed[1])
    cots[1] = links.gather_other(after(came_cot, fw[1][4]))
    back[1] = cotangents(1, cots[1], fw[1][4])
    stats = [jnp.stack([fw[r][5][0], back[r][2]]) for r in range(2)]
    stats = links.sum_stats(stats[0], stats[1])
    sent_out, came_out = links.reduce_other(project_out(after(fw[1][4], back[1][2])))
    inv, rks = [], []
    for r in range(2):
        scale = lax.rsqrt(stats[r][0] / inner + EPS)
        kappa = scale * scale * (stats[r][1] / inner)
        inv.append(scale)
        rks.append(
            jnp.concatenate(
                [jnp.broadcast_to(scale[:, None], (ROW_LEN, 128)), jnp.broadcast_to(kappa[:, None], (ROW_LEN, 128))],
                axis=1,
            )
        )
    grads_1 = out_gradients(1, back[1][0], fw[1][4], inv[1])
    grads_0 = out_gradients(0, back[0][0], fw[0][4], inv[0])
    down_total, up_total = [a + b for a, b in zip(grads_0, grads_1)]
    up_sum, out_down_sum = lax.psum((up_total.astype(BF16), down_total.astype(BF16)), "dp")

    gm_1 = after(back[1][1], sent_out, down_total, up_total)
    ext_1, *in_1 = backward(1, gm_1)
    sent_in, came_in = links.reduce_other(project_in(after(ext_1, came_out)))
    gm_0 = after(back[0][1], sent_in)
    ext_0, *in_0 = backward(0, gm_0)
    ext_0, up_sum, out_down_sum = lax.optimization_barrier((after(ext_0, came_in), up_sum, out_down_sum))
    in_up_total, in_down_total = [(a + b).T for a, b in zip(in_1, in_0)]
    in_chain = FactorSum(in_down_total, in_up_total, up_sum.astype(F32))

    whole_out = project_out(in_chain.cover(after(fw[0][4], ext_0)))
    whole_in = project_in(in_chain.cover(after(ext_0, whole_out)))
    out_sum = links.reduce_own(whole_out, in_chain.cover(after(came_out, whole_in)))
    output = (residual + links.mine(inv[0])[:, None] * out_sum).astype(BF16)
    grad_normed = links.reduce_own(whole_in, in_chain.cover(after(came_in, output)))
    scaled = grad_normed * norm_gain
    inner_sum = jnp.sum(scaled * residual, axis=1, keepdims=True) / model
    grad_tokens = cotangent.astype(F32) + inv_rms * scaled - residual * inv_rms**3 * inner_sum
    in_down_sum, in_up_sum, out_up_sum = in_chain.finish()
    out_up_sum, out_down_sum = out_up_sum.T, out_down_sum.astype(F32)
    in_up_sum = in_up_sum.T
    return (
        output,
        grad_tokens,
        in_down_sum.reshape(model, adapters, rank),
        in_up_sum.reshape(adapters, rank, 2, width),
        out_down_sum.reshape(width, adapters, rank),
        out_up_sum.reshape(adapters, rank, model),
    )


def solution(mesh):
    return jax.shard_map(
        on_device,
        mesh=mesh,
        in_specs=(
            P(("dp", "tensor"), None), P(("dp", "tensor"), None), P(), P(), P(), P(),
            P(None, None, "tensor"), P(), P(None, "tensor"), P(None, "tensor"), P(), P(None, "tensor"),
            P("tensor"), P("tensor", None), P(), P(None, None, None, "tensor"), P("tensor", None, None), P(),
        ),
        out_specs=(
            P(("dp", "tensor"), None), P(("dp", "tensor"), None), P(),
            P(None, None, None, "tensor"), P("tensor", None, None), P(),
        ),
        check_vma=False,
    )
```
